32 devices in a mesh: seq: 4 (over y, x), head: 8 (over z, core).
Axes of the slice: x: 2, y: 2, z: 4, core: 2. Of those that a mesh axis runs over, the one named last changes fastest.
Arguments:
- hidden_in: bfloat16 [16384, 1536], P('seq'), may hold values from -6 to 6
- norm_gain: float32 [1536], replicated, may hold values from 0.1 to 1.9
- gate_proj: bfloat16 [1536, 1024], P(None, 'head'), may hold values from -0.15625 to 0.15625
- value_proj: bfloat16 [1536, 1024], P(None, 'head'), may hold values from -0.21875 to 0.21875
- state_proj: bfloat16 [1536, 256], replicated, may hold values from -0.15625 to 0.15625
- step_proj: bfloat16 [1536, 16], P(None, 'head'), may hold values from -0.15625 to 0.15625
- conv_value: float32 [4, 1024], P(None, 'head'), may hold values from -3 to 3
- conv_value_bias: float32 [1024], P('head'), may hold values from -3 to 3
- conv_state: float32 [4, 256], replicated, may hold values from -3 to 3
- conv_state_bias: float32 [256], replicated, may hold values from -3 to 3
- step_bias: float32 [16], P('head'), may hold values from -1 to 1
- decay_rate: float32 [16], P('head'), may hold values from 3.0517578e-05 to 0.03
- skip_gain: float32 [16], P('head'), may hold values from 0.1 to 1.9
- mix_gain: float32 [1024], P('head'), may hold values from 0.1 to 1.9
- out_proj: bfloat16 [1024, 1536], P('head'), may hold values from -0.25 to 0.25
- out_grad: bfloat16 [16384, 1536], P('seq'), may hold values from -6 to 6
Outputs:
- block_out: bfloat16 [16384, 1536], P('seq', 'head')
- grad_input: float32 [16384, 1536], P('seq', 'head')
- grad_norm_gain: float32 [1536], P('head')
- grad_gate_proj: float32 [1536, 1024], P(None, 'head')
- grad_value_proj: float32 [1536, 1024], P(None, 'head')
- grad_state_proj: float32 [1536, 256], P('head')
- grad_step_proj: float32 [1536, 16], P(None, 'head')
- grad_conv_value: float32 [4, 1024], P(None, 'head')
- grad_conv_value_bias: float32 [1024], P('head')
- grad_conv_state: float32 [4, 256], replicated
- grad_conv_state_bias: float32 [256], replicated
- grad_step_bias: float32 [16], P('head')
- grad_decay_rate: float32 [16], P('head')
- grad_skip_gain: float32 [16], P('head')
- grad_mix_gain: float32 [1024], P('head')
- grad_out_proj: float32 [1024, 1536], P('head')
The draws below stay inside these ranges and needn't reach their ends.
All inputs are finite; a program needn't handle non-finite values.
Results may differ from the reference program's by a relative error of at most 0.012.
The reference program's roundings to bfloat16 on the way count: a program that leaves them out, or rounds other values in their place, can miss the bound.
Values may be sent and summed in bfloat16 or wider, within the bound.
No kernel may reach another device: no remote copies, remote signals or barrier semaphores. Data moves between devices by JAX's collectives and lax.ppermute only.
A program may use at most 384 MiB of HBM per device.

```python
import math
import jax
import jax.numpy as jnp
from jax import lax

D = 1536
HEAD_DEV = 2
P_SIZE = 64
N_STATE = 128
KW = 4
SPAN = 256
HEADS = 16
INNER = 1024
TOKENS = 16384
N_HEAD = 8


def raised(values, stream_key, source, target, blocks, factor):
    owner, partner = [(jnp.arange(values.shape[position]) // (values.shape[position] // blocks)).reshape([-1 if axis == position else 1 for axis in range(values.ndim)]) for position in (source, target)]
    chosen = jax.random.permutation(stream_key, blocks)[partner]
    strong = (owner == chosen) | (owner == (partner + blocks // 2) % blocks)
    return jnp.where(strong, factor * values, values)


def block_levels(stream_key, shape, cuts, smallest, high):
    loudness = 1.0
    for axis_at, shards_of in cuts:
        draws = jax.random.uniform(jax.random.fold_in(jax.random.fold_in(stream_key, 6), axis_at), (shards_of,), jnp.float32, smallest / len(cuts), high / len(cuts))
        loudness = loudness * jnp.repeat(jnp.exp(draws), shape[axis_at] // shards_of).reshape((-1,) + (1,) * (len(shape) - 1 - axis_at))
    return loudness


def noise(own_key, shape, scale, reach, cuts=(), held_as=jnp.bfloat16):
    gain = block_levels(own_key, shape, cuts, -0.22, 0.18) if cuts else 1.0
    result = jax.random.normal(own_key, shape, jnp.float32) * scale * gain
    return jnp.minimum(jnp.maximum(result, -reach), reach).astype(held_as)


def heavy_noise(rng, dims, deviation, reach, cuts, heavy, dtype=jnp.bfloat16):
    entries = deviation * jax.random.normal(rng, dims, jnp.float32)
    if cuts:
        entries = entries * block_levels(rng, dims, cuts, -0.22, 0.18)
    return jnp.clip(raised(entries, jax.random.fold_in(rng, 3), *heavy), -reach, reach).astype(dtype)


def setup_inputs(seed: int = 0) -> dict:
    arg_keys = jax.random.split(jax.random.key(seed), 17)
    return {
        "hidden_in": noise(arg_keys[0], (TOKENS, D), 1.0, 6.0, ((0, 4),)),
        "norm_gain": jnp.clip(1.0 + 0.18 * jax.random.normal(arg_keys[1], (D,), jnp.float32), 0.1, 1.9),
        "gate_proj": noise(arg_keys[2], (D, INNER), D ** -0.5, 0.15625, ((1, 8),)),
        "value_proj": heavy_noise(arg_keys[3], (D, INNER), D ** -0.5, 0.21875, ((1, 8),), (1, 0, 8, 2.0)),
        "state_proj": noise(arg_keys[4], (D, 2 * N_STATE), D ** -0.5, 0.15625),
        "step_proj": noise(arg_keys[5], (D, HEADS), D ** -0.5, 0.15625, ((1, 8),)),
        "conv_value": noise(arg_keys[6], (KW, INNER), 0.5, 3.0, ((1, 8),), jnp.float32),
        "conv_value_bias": noise(arg_keys[7], (INNER,), 0.5, 3.0, ((0, 8),), jnp.float32),
        "conv_state": noise(arg_keys[8], (KW, 2 * N_STATE), 0.5, 3.0, (), jnp.float32),
        "conv_state_bias": noise(arg_keys[9], (2 * N_STATE,), 0.5, 3.0, (), jnp.float32),
        "step_bias": jnp.clip(jax.random.uniform(arg_keys[10], (HEADS,), jnp.float32, -1.0, 1.0) * block_levels(arg_keys[10], (HEADS,), ((0, 8),), -0.4, 0.0), -1.0, 1.0),
        "decay_rate": jnp.clip(jnp.exp(math.log(0.03) - 6.89065 * jax.random.uniform(arg_keys[11], (HEADS,), jnp.float32) ** block_levels(arg_keys[11], (HEADS,), ((0, 8),), -0.2, 0.2)), 3.0517578125e-05, 0.03),
        "skip_gain": jnp.clip(1.0 + 0.18 * jax.random.normal(arg_keys[12], (HEADS,), jnp.float32), 0.1, 1.9),
        "mix_gain": jnp.clip(1.0 + 0.18 * jax.random.normal(arg_keys[13], (INNER,), jnp.float32), 0.1, 1.9),
        "out_proj": heavy_noise(arg_keys[14], (INNER, D), INNER ** -0.5, 0.25, ((0, 8),), (0, 1, 8, 2.0)),
        "out_grad": noise(arg_keys[15], (TOKENS, D), 1.0, 6.0, ((0, 4),)),
    }


epsilon = 1e-05
highest = lax.Precision.HIGHEST

def span_step(carried, inputs):
    values, keys_in, queries, widths, log_decay = inputs
    running = jnp.cumsum(log_decay, axis=0)
    scores = jnp.dot(queries, keys_in.T, precision=highest)
    length_here = values.shape[0]
    lower = jnp.arange(length_here)[:, None] >= jnp.arange(length_here)[None, :]
    running_h = running.T
    spread = jnp.where(lower[None, :, :], running_h[:, :, None] - running_h[:, None, :], -jnp.inf)
    weights = scores[None, :, :] * jnp.exp(spread) * widths.T[:, None, :]
    values_h = jnp.transpose(values, (1, 0, 2))
    outputs_h = jnp.einsum('hij,hjp->hip', weights, values_h, precision=highest)
    outputs = jnp.transpose(outputs_h, (1, 0, 2))
    outputs = outputs + jnp.exp(running)[:, :, None] * jnp.einsum('in,hpn->ihp', queries, carried, precision=highest)
    tails = jnp.exp(running[-1][None, :] - running) * widths
    fresh = jnp.exp(running[-1])[:, None, None] * carried + jnp.einsum('hjp,jn->hpn', values_h * tails.T[:, :, None], keys_in, precision=highest)
    return (fresh, outputs)

def mixer(conv_out, step_raw, step_bias, decay_rate, skip_gain, gate_in, mix_gain):
    active = jax.nn.silu(conv_out)
    values = active[:, :INNER].reshape(TOKENS, HEADS, P_SIZE)
    keys_in = active[:, INNER:INNER + N_STATE]
    queries = active[:, INNER + N_STATE:]
    widths = jax.nn.softplus(step_raw + step_bias[None, :])
    log_decay = -decay_rate[None, :] * widths
    blocks_all = TOKENS // SPAN
    inputs = (values.reshape(blocks_all, SPAN, HEADS, P_SIZE), keys_in.reshape(blocks_all, SPAN, N_STATE), queries.reshape(blocks_all, SPAN, N_STATE), widths.reshape(blocks_all, SPAN, HEADS), log_decay.reshape(blocks_all, SPAN, HEADS))
    anchor = jnp.zeros((HEADS, P_SIZE, N_STATE), jnp.float32)
    final_state, outputs = lax.scan(jax.checkpoint(span_step), anchor, inputs)
    mixed = outputs.reshape(TOKENS, HEADS, P_SIZE) + skip_gain[None, :, None] * values
    gated = mixed.reshape(TOKENS, INNER) * jax.nn.silu(gate_in)
    scale_gate = lax.rsqrt(lax.optimization_barrier(jnp.mean(gated * gated, axis=1, keepdims=True)) + epsilon)
    return gated * scale_gate * mix_gain[None, :]

def prenorm(hidden, norm_gain):
    scale_in = lax.rsqrt(lax.optimization_barrier(jnp.mean(hidden * hidden, axis=1, keepdims=True)) + epsilon)
    return hidden * scale_in * norm_gain[None, :]

def convolve(extended, kernel, offset_row):
    total = offset_row[None, :] + kernel[0][None, :] * extended[0:TOKENS]
    for tap_index in range(1, KW):
        total = total + kernel[tap_index][None, :] * extended[tap_index:tap_index + TOKENS]
    return total

def out_group(total, pieces):
    term = jnp.dot(pieces[0], pieces[1], preferred_element_type=jnp.float32).astype(jnp.bfloat16)
    term = lax.optimization_barrier(term)
    return (total + term.astype(jnp.float32), None)

def input_group(total, pieces):
    gate_part, value_part, step_part, gate_rows_w, value_rows_w, step_rows_w = pieces
    term = (jnp.dot(gate_part, gate_rows_w.T, preferred_element_type=jnp.float32) + jnp.dot(value_part, value_rows_w.T, preferred_element_type=jnp.float32) + jnp.dot(step_part, step_rows_w.T, preferred_element_type=jnp.float32)).astype(jnp.bfloat16)
    term = lax.optimization_barrier(term)
    return (total + term.astype(jnp.float32), None)

def split_columns(matrix, width):
    return jnp.swapaxes(matrix.reshape(matrix.shape[0], N_HEAD, width), 0, 1)

def reference(hidden_in, norm_gain, gate_proj, value_proj, state_proj, step_proj, conv_value, conv_value_bias, conv_state, conv_state_bias, step_bias, decay_rate, skip_gain, mix_gain, out_proj, out_grad):
    group_width = INNER // N_HEAD
    hidden = hidden_in.astype(jnp.float32)
    normed, norm_back = jax.vjp(prenorm, hidden, norm_gain)
    projected = normed.astype(jnp.bfloat16)
    gate_in = jnp.dot(projected, gate_proj, preferred_element_type=jnp.float32)
    stream = jnp.concatenate([jnp.dot(projected, value_proj, preferred_element_type=jnp.float32).astype(jnp.bfloat16), jnp.dot(projected, state_proj, preferred_element_type=jnp.float32).astype(jnp.bfloat16)], axis=1)
    step_raw = jnp.dot(projected, step_proj, preferred_element_type=jnp.float32)
    extended = jnp.concatenate([jnp.zeros((KW - 1, stream.shape[1]), jnp.float32), stream.astype(jnp.float32)], axis=0)
    kernel = jnp.concatenate([conv_value, conv_state], axis=1)
    offset_row = jnp.concatenate([conv_value_bias, conv_state_bias])
    conv_out, conv_back = jax.vjp(convolve, extended, kernel, offset_row)
    normed_gate, mixer_back = jax.vjp(mixer, conv_out, step_raw, step_bias, decay_rate, skip_gain, gate_in, mix_gain)
    gated_rows = normed_gate.astype(jnp.bfloat16)
    branch_out, unused = lax.scan(out_group, jnp.zeros((TOKENS, D), jnp.float32), (split_columns(gated_rows, group_width), out_proj.reshape(N_HEAD, group_width, D)))
    block_out = (branch_out + hidden).astype(jnp.bfloat16)
    grad_gated = jnp.dot(out_grad, out_proj.T, preferred_element_type=jnp.float32)
    grad_out_proj = jnp.dot(gated_rows.T, out_grad, preferred_element_type=jnp.float32)
    grad_conv, grad_step_raw, grad_step_bias, grad_decay, grad_skip, grad_gate_in, grad_mix_gain = mixer_back(grad_gated)
    grad_ext, grad_kernel, grad_offset = conv_back(grad_conv)
    grad_stream = grad_ext[KW - 1:]
    grad_value16 = grad_stream[:, :INNER].astype(jnp.bfloat16)
    grad_state16 = grad_stream[:, INNER:].astype(jnp.bfloat16)
    grad_gate16 = grad_gate_in.astype(jnp.bfloat16)
    grad_step16 = grad_step_raw.astype(jnp.bfloat16)
    grad_gate_proj = jnp.dot(projected.T, grad_gate16, preferred_element_type=jnp.float32)
    grad_value_proj = jnp.dot(projected.T, grad_value16, preferred_element_type=jnp.float32)
    grad_state_proj = jnp.dot(projected.T, grad_state16, preferred_element_type=jnp.float32)
    grad_step_proj = jnp.dot(projected.T, grad_step16, preferred_element_type=jnp.float32)
    pieces = (split_columns(grad_gate16, group_width), split_columns(grad_value16, group_width), split_columns(grad_step16, HEAD_DEV), split_columns(gate_proj, group_width), split_columns(value_proj, group_width), split_columns(step_proj, HEAD_DEV))
    grad_projected, unused_too = lax.scan(input_group, jnp.zeros((TOKENS, D), jnp.float32), pieces)
    grad_projected = grad_projected + jnp.dot(grad_state16, state_proj.T, preferred_element_type=jnp.float32)
    grad_hidden, grad_norm_gain = norm_back(grad_projected)
    grad_input = grad_hidden + out_grad.astype(jnp.float32)
    return (block_out, grad_input, grad_norm_gain, grad_gate_proj, grad_value_proj, grad_state_proj, grad_step_proj, grad_kernel[:, :INNER], grad_offset[:INNER], grad_kernel[:, INNER:], grad_offset[INNER:], grad_step_bias, grad_decay, grad_skip, grad_mix_gain, grad_out_proj)
```

```python
from functools import partial

import jax
import jax.numpy as jnp
from jax import lax
from jax.experimental import pallas as pl
from jax.experimental.pallas import tpu as pltpu
from jax.sharding import PartitionSpec as P


SPAN = 256
epsilon = 1e-05
f32 = jnp.float32
bf16 = jnp.bfloat16


def mm(a, b):
    return jnp.dot(a, b, preferred_element_type=f32)


def mm_nt(a, b):
    return lax.dot_general(a, b, (((1,), (1,)), ((), ())), preferred_element_type=f32)


def mm_tn(a, b):
    return lax.dot_general(a, b, (((0,), (0,)), ((), ())), preferred_element_type=f32)


def halves(x):
    high = x.astype(bf16)
    return jnp.concatenate([high, (x - high.astype(f32)).astype(bf16)], axis=1)


def two(x):
    high = x.astype(bf16)
    return high, (x - high.astype(f32)).astype(bf16)


def left_terms(x, axis):
    high, low = two(x)
    return jnp.concatenate([high, high, low], axis=axis)


def right_terms(x):
    high, low = two(x)
    return jnp.concatenate([high, low, high], axis=0)


def wide_terms(x):
    high, low = two(x)
    return jnp.concatenate([high, low, high], axis=1)


def folded(x):
    width = x.shape[1] // 2
    return x[:, :width] + x[:, width:]


def logistic(x):
    return 1.0 / (1.0 + jnp.exp(-x))


def softplus(x):
    return jnp.maximum(x, 0.0) + jnp.log1p(jnp.exp(-jnp.abs(x)))


def iota(shape, axis):
    return lax.broadcasted_iota(jnp.int32, shape, axis)


def params(grid_axes=1, limit=56 << 20):
    return pltpu.CompilerParams(
        dimension_semantics=("arbitrary",) * grid_axes, vmem_limit_bytes=limit
    )


def spec(shape, index):
    return pl.BlockSpec(shape, index)


def whole_block(array):
    rank = array.ndim
    return pl.BlockSpec(array.shape, lambda *i: (0,) * rank)


def project_kernel(
    hidden_ref, gain_ref, gate_ref, value_ref, state_ref, step_ref,
    projected_ref, gate_out, stream_out, step_out, scale_out, weights,
):
    @pl.when(pl.program_id(0) == 0)
    def _():
        weights[:, 0:128] = gate_ref[...]
        weights[:, 128:256] = value_ref[...]
        weights[:, 256:512] = state_ref[...]
        weights[:, 512:640] = step_ref[...]

    hidden = hidden_ref[...].astype(f32)
    scale = lax.rsqrt(jnp.mean(hidden * hidden, axis=1, keepdims=True) + epsilon)
    projected = (hidden * scale * gain_ref[...]).astype(bf16)
    projected_ref[...] = projected
    scale_out[...] = jnp.broadcast_to(scale, scale_out.shape)
    result = mm(projected, weights[...])
    gate_out[...] = result[:, 0:128]
    stream_out[...] = result[:, 128:512].astype(bf16)
    step_out[...] = result[:, 512:640]


def project(hidden_in, norm_gain, gate_proj, value_proj, state_proj, step_wide):
    rows, width = hidden_in.shape
    span = 512
    row = lambda i: (i, 0)
    gain = norm_gain[None, :]
    return pl.pallas_call(
        project_kernel,
        grid=(rows // span,),
        in_specs=[
            spec((span, width), row), whole_block(gain), whole_block(gate_proj),
            whole_block(value_proj), whole_block(state_proj), whole_block(step_wide),
        ],
        out_specs=[
            spec((span, width), row), spec((span, 128), row), spec((span, 384), row),
            spec((span, 128), row), spec((span, 128), row),
        ],
        out_shape=[
            jax.ShapeDtypeStruct((rows, width), bf16),
            jax.ShapeDtypeStruct((rows, 128), f32),
            jax.ShapeDtypeStruct((rows, 384), bf16),
            jax.ShapeDtypeStruct((rows, 128), f32),
            jax.ShapeDtypeStruct((rows, 128), f32),
        ],
        scratch_shapes=[pltpu.VMEM((width, 640), bf16)],
        compiler_params=params(),
        cost_estimate=pl.CostEstimate(
            flops=2 * rows * width * 640, bytes_accessed=rows * width * 4, transcendentals=0
        ),
        name="project",
    )(hidden_in, gain, gate_proj, value_proj, state_proj, step_wide)


def convolved(ext, taps, bias):
    span = SPAN
    total = bias + taps[0:1] * ext[5 : 5 + span]
    for tap in range(1, 4):
        total = total + taps[tap : tap + 1] * ext[5 + tap : 5 + tap + span]
    return total


def running_sums(log_decay):
    span = log_decay.shape[0]
    lower = (iota((span, span), 0) >= iota((span, span), 1)).astype(bf16)
    return folded(mm(lower, halves(log_decay)))


def decay_matrix(running, running_rows, head):
    span = running.shape[0]
    at = 64 * head
    spread = running[:, at : at + 1] - running_rows[at : at + 1, :]
    return jnp.exp(jnp.where(iota((span, span), 0) >= iota((span, span), 1), spread, -jnp.inf))


def forward_kernel(
    stream_ref, edge_ref, step_ref, taps_ref, bias_ref, step_bias_ref, rate_ref, skip_ref,
    mixed_out, query_out, reach_out, states_out,
    ext, state, offset,
):
    span = SPAN
    first = pl.program_id(0) == 0

    @pl.when(first)
    def _():
        ext[0:8] = edge_ref[...].astype(f32)
        state[...] = jnp.zeros_like(state)
        offset[...] = jnp.zeros_like(offset)

    ext[8 : 8 + span] = stream_ref[...].astype(f32)
    conv = convolved(ext, taps_ref[...], bias_ref[...])
    ext[0:8] = ext[span : span + 8]
    active = conv * logistic(conv)
    values = active[:, 0:128]
    keys = active[:, 128:256]
    queries = active[:, 256:384]
    widths = softplus(step_ref[...] + step_bias_ref[...])
    running = running_sums(-rate_ref[...] * widths)
    running_rows = running.T
    last = running[span - 1 : span, :]
    fed = widths * values
    fed_terms = right_terms(fed)
    query_terms = left_terms(queries, 1)
    scores = mm_nt(query_terms, wide_terms(keys))
    low = iota((span, 128), 1) < 64
    heads = [
        mm(left_terms(scores * decay_matrix(running, running_rows, head), 1), fed_terms)
        for head in range(2)
    ]
    before = state[...]
    mixed = jnp.where(low, heads[0], heads[1])
    mixed = mixed + jnp.exp(running) * mm_nt(query_terms, wide_terms(before))
    mixed_out[...] = mixed + skip_ref[...] * values
    query_out[...] = queries
    reach_out[...] = running + offset[0:1]
    offset[...] = offset[...] + last
    tails = left_terms(jnp.exp(last - running) * fed, 0)
    after = jnp.exp(running_rows[:, span - 1 : span]) * before + mm_tn(tails, right_terms(keys))
    state[...] = after
    states_out[0] = after


def scan_forward(stream, edge, step, taps, bias, step_bias, rate, skip):
    rows = stream.shape[0]
    span = SPAN
    count = rows // span
    row = lambda i: (i, 0)
    return pl.pallas_call(
        forward_kernel,
        grid=(count,),
        in_specs=[
            spec((span, 384), row), whole_block(edge), spec((span, 128), row), whole_block(taps),
            whole_block(bias), whole_block(step_bias), whole_block(rate), whole_block(skip),
        ],
        out_specs=[
            spec((span, 128), row), spec((span, 128), row), spec((span, 128), row),
            spec((1, 128, 128), lambda i: (i, 0, 0)),
        ],
        out_shape=[
            jax.ShapeDtypeStruct((rows, 128), f32),
            jax.ShapeDtypeStruct((rows, 128), f32),
            jax.ShapeDtypeStruct((rows, 128), f32),
            jax.ShapeDtypeStruct((count, 128, 128), f32),
        ],
        scratch_shapes=[
            pltpu.VMEM((span + 8, 384), f32), pltpu.VMEM((128, 128), f32), pltpu.VMEM((8, 128), f32),
        ],
        compiler_params=params(),
        cost_estimate=pl.CostEstimate(
            flops=count * 2 * span * span * 600, bytes_accessed=rows * 128 * 20, transcendentals=0
        ),
        name="scan_forward",
    )(stream, edge, step, taps, bias, step_bias, rate, skip)


def join_kernel(
    mixed_ref, query_ref, reach_ref, gate_ref, grad_ref, carried_ref, gain_ref, mixed_out, sums_out
):
    inner = mm_nt(left_terms(query_ref[...], 1), wide_terms(carried_ref[...]))
    mixed = mixed_ref[...] + jnp.exp(reach_ref[...]) * inner
    mixed_out[...] = mixed
    gate = gate_ref[...]
    gated = mixed * (gate * logistic(gate))
    sums_out[0:1, :] = jnp.sum((gated * gated).T, axis=0, keepdims=True)
    sums_out[1:2, :] = jnp.sum((grad_ref[...] * gain_ref[...] * gated).T, axis=0, keepdims=True)


def join(mixed, query, reach, gate, grad, carried, gain):
    rows = mixed.shape[0]
    block = 512
    row = lambda i: (i, 0)
    blocks = spec((block, 128), row)
    return pl.pallas_call(
        join_kernel,
        grid=(rows // block,),
        in_specs=[blocks] * 5 + [whole_block(carried), whole_block(gain)],
        out_specs=[blocks, spec((2, block), lambda i: (0, i))],
        out_shape=[
            jax.ShapeDtypeStruct((rows, 128), f32), jax.ShapeDtypeStruct((2, rows), f32),
        ],
        compiler_params=params(),
        cost_estimate=pl.CostEstimate(
            flops=2 * rows * 128 * 128, bytes_accessed=rows * 128 * 22, transcendentals=0
        ),
        name="join",
    )(mixed, query, reach, gate, grad, carried, gain)


def gate_kernel(
    inner_width,
    mixed_ref, query_ref, reach_ref, gate_ref, grad_ref, sums_ref, gain_ref,
    rows_out, gate_out, mixed_grad_out, gain_out, incoming_out,
):
    @pl.when(pl.program_id(0) == 0)
    def _():
        gain_out[...] = jnp.zeros_like(gain_out)
        incoming_out[...] = jnp.zeros_like(incoming_out)

    block = mixed_ref.shape[0]
    square = jnp.broadcast_to(sums_ref[0:1, :], (128, block)).T
    product = jnp.broadcast_to(sums_ref[1:2, :], (128, block)).T
    scale = lax.rsqrt(square / inner_width + epsilon)
    gate = gate_ref[...]
    chance = logistic(gate)
    act = gate * chance
    mixed = mixed_ref[...]
    hat = mixed * act * scale
    rows_out[...] = (hat * gain_ref[...]).astype(bf16)
    grad = grad_ref[...]
    gain_out[...] += jnp.sum(grad * hat, axis=0, keepdims=True)
    pre = scale * (grad * gain_ref[...] - hat * (product * scale / inner_width))
    mixed_grad = pre * act
    mixed_grad_out[...] = mixed_grad
    gate_out[...] = (pre * mixed * (chance * (1.0 + gate * (1.0 - chance)))).astype(bf16)
    incoming_out[...] += mm_tn(
        left_terms(jnp.exp(reach_ref[...]) * mixed_grad, 0), right_terms(query_ref[...])
    )


def gate_step(mixed, query, reach, gate, grad, sums, gain, inner_width):
    rows = mixed.shape[0]
    block = 512
    row = lambda i: (i, 0)
    blocks = spec((block, 128), row)
    return pl.pallas_call(
        partial(gate_kernel, inner_width),
        grid=(rows // block,),
        in_specs=[blocks] * 5 + [spec((2, block), lambda i: (0, i)), whole_block(gain)],
        out_specs=[
            blocks, blocks, blocks, spec((1, 128), lambda i: (0, 0)),
            spec((128, 128), lambda i: (0, 0)),
        ],
        out_shape=[
            jax.ShapeDtypeStruct((rows, 128), bf16),
            jax.ShapeDtypeStruct((rows, 128), bf16),
            jax.ShapeDtypeStruct((rows, 128), f32),
            jax.ShapeDtypeStruct((1, 128), f32),
            jax.ShapeDtypeStruct((128, 128), f32),
        ],
        compiler_params=params(),
        cost_estimate=pl.CostEstimate(
            flops=2 * rows * 128 * 128, bytes_accessed=rows * 128 * 26, transcendentals=0
        ),
        name="gate_step",
    )(mixed, query, reach, gate, grad, sums, gain)


def head_sums(x):
    same = (iota((128, 128), 0) < 64) == (iota((128, 128), 1) < 64)
    ones = same.astype(bf16)
    high = x.astype(bf16)
    return mm(high, ones) + mm((x - high.astype(f32)).astype(bf16), ones)


def backward_kernel(
    stream_ref, before_ref, edge_ref, step_ref, taps_ref, bias_ref, step_bias_ref, rate_ref,
    skip_ref, mixed_ref, grad_ref, reach_ref, start_ref, end_ref, carried_ref, arriving_ref,
    stream_grad_out, tail_out, head_out, sums_out,
    ext, grads, state_grad,
):
    span = SPAN
    count = pl.num_programs(0)
    chunk = count - 1 - pl.program_id(0)

    @pl.when(pl.program_id(0) == 0)
    def _():
        state_grad[...] = arriving_ref[...]
        grads[span : span + 8] = jnp.zeros_like(grads[span : span + 8])
        sums_out[...] = jnp.zeros_like(sums_out)

    @pl.when(chunk == 0)
    def _():
        ext[0:8] = edge_ref[...].astype(f32)

    @pl.when(chunk > 0)
    def _():
        ext[0:8] = before_ref[8:16].astype(f32)

    ext[8 : 8 + span] = stream_ref[...].astype(f32)
    taps = taps_ref[...]
    conv = convolved(ext, taps, bias_ref[...])
    chance = logistic(conv)
    active = conv * chance
    slope = chance * (1.0 + conv * (1.0 - chance))
    values = active[:, 0:128]
    keys = active[:, 128:256]
    queries = active[:, 256:384]
    keys16 = keys.astype(bf16)
    step = step_ref[...] + step_bias_ref[...]
    rate = rate_ref[...]
    widths = softplus(step)
    running = running_sums(-rate * widths)
    running_rows = running.T
    last = running[span - 1 : span, :]
    fed = widths * values
    fed16 = fed.astype(bf16)
    grad = grad_ref[...]
    grad16 = grad.astype(bf16)
    scores = mm_nt(queries.astype(bf16), keys16)
    low = iota((span, 128), 1) < 64
    grad_turned = pltpu.roll(grad, 64, 1)
    fed_turned = pltpu.roll(fed, 64, 1)
    score_grad = None
    fed_grads = []
    for head in range(2):
        decay = decay_matrix(running, running_rows, head)
        mine = low == (head == 0)
        grad_high, grad_low = two(jnp.where(mine, grad, grad_turned))
        left = [jnp.where(low, grad_high, grad_low), jnp.where(low, grad_high, 0)]
        right = two(jnp.where(mine, fed, fed_turned))
        part = mm_nt(jnp.concatenate(left, axis=1), jnp.concatenate(right, axis=1)) * decay
        score_grad = part if score_grad is None else score_grad + part
        fed_grads.append(mm_tn((scores * decay).astype(bf16), grad16))

    offset = (reach_ref[span - 8 : span, :] - running[span - 8 : span, :]).T[:, 7:8]
    carried = jnp.exp(offset) * carried_ref[...]
    before = jnp.where(chunk > 0, start_ref[0], 0.0) + carried
    last_rows = jnp.exp(running_rows[:, span - 1 : span])
    after = end_ref[0] + last_rows * carried
    after_grad = state_grad[...]
    tail = jnp.exp(last - running)
    reached = jnp.exp(running) * grad
    query_terms = right_terms(queries)
    fed_grad = jnp.where(low, fed_grads[0], fed_grads[1])
    fed_grad = fed_grad + tail * mm_nt(keys16, after_grad.astype(bf16))
    score_high, score_low = two(score_grad)
    query_grad = mm(
        jnp.concatenate([score_high, score_high, score_low], axis=1), right_terms(keys)
    ) + mm(left_terms(reached, 1), right_terms(before))
    key_grad = mm_tn(
        jnp.concatenate([score_high, score_high, score_low], axis=0), query_terms
    ) + mm(left_terms(tail * fed, 1), right_terms(after_grad))
    state_grad[...] = last_rows * after_grad + mm_tn(left_terms(reached, 0), query_terms)
    value_grad = widths * fed_grad + skip_ref[...] * grad

    mixed = mixed_ref[...] - skip_ref[...] * values
    balance = head_sums(grad16.astype(f32) * mixed - fed16.astype(f32) * fed_grad)
    upper = (iota((span, span), 0) <= iota((span, span), 1)).astype(bf16)
    boundary = head_sums(
        jnp.broadcast_to(jnp.sum((after_grad * after).T, axis=0, keepdims=True), (8, 128))
    )
    decay_grad = folded(mm(upper, halves(balance))) + boundary[0:1]
    width_grad = head_sums(values * fed_grad) - rate * decay_grad
    step_grad = width_grad * logistic(step)
    sums_out[0:1, 384:512] += jnp.sum(step_grad, axis=0, keepdims=True)
    sums_out[1:2, 384:512] += jnp.sum(-widths * decay_grad, axis=0, keepdims=True)
    sums_out[2:3, 384:512] += jnp.sum(grad * values, axis=0, keepdims=True)

    conv_grad = jnp.concatenate([value_grad, key_grad, query_grad], axis=1) * slope
    grads[0:span] = conv_grad
    for tap in range(4):
        sums_out[tap : tap + 1, 0:384] += jnp.sum(
            conv_grad * ext[5 + tap : 5 + tap + span], axis=0, keepdims=True
        )
    sums_out[4:5, 0:384] += jnp.sum(conv_grad, axis=0, keepdims=True)
    stream_grad = taps[3:4] * conv_grad
    for tap in range(3):
        stream_grad = stream_grad + taps[tap : tap + 1] * grads[3 - tap : 3 - tap + span]
    high = stream_grad.astype(bf16)
    stream_grad_out[:, 0:384] = high
    stream_grad_out[:, 384:512] = step_grad.astype(bf16)
    stream_grad_out[:, 512:768] = (stream_grad - high.astype(f32))[:, 128:384].astype(bf16)

    @pl.when(pl.program_id(0) == 0)
    def _():
        tail_out[...] = stream_grad[span - 8 :]

    head_out[...] = conv_grad[0:8]
    grads[span : span + 8] = conv_grad[0:8]


def scan_backward(
    stream, edge, step, taps, bias, step_bias, rate, skip, mixed, grad, reach, states, carried,
    arriving,
):
    rows = stream.shape[0]
    span = SPAN
    count = rows // span
    row = lambda i: (count - 1 - i, 0)
    fixed = lambda i: (0, 0)
    return pl.pallas_call(
        backward_kernel,
        grid=(count,),
        in_specs=[
            spec((span, 384), row),
            spec((16, 384), lambda i: (jnp.maximum((count - 1 - i) * (span // 16) - 1, 0), 0)),
            whole_block(edge), spec((span, 128), row), whole_block(taps), whole_block(bias),
            whole_block(step_bias), whole_block(rate), whole_block(skip), spec((span, 128), row),
            spec((span, 128), row), spec((span, 128), row),
            spec((1, 128, 128), lambda i: (jnp.maximum(count - 2 - i, 0), 0, 0)),
            spec((1, 128, 128), lambda i: (count - 1 - i, 0, 0)),
            whole_block(carried), whole_block(arriving),
        ],
        out_specs=[
            spec((span, 768), row), spec((8, 384), fixed), spec((8, 384), fixed),
            spec((8, 512), fixed),
        ],
        out_shape=[
            jax.ShapeDtypeStruct((rows, 768), bf16),
            jax.ShapeDtypeStruct((8, 384), f32),
            jax.ShapeDtypeStruct((8, 384), f32),
            jax.ShapeDtypeStruct((8, 512), f32),
        ],
        scratch_shapes=[
            pltpu.VMEM((span + 8, 384), f32), pltpu.VMEM((span + 8, 384), f32),
            pltpu.VMEM((128, 128), f32),
        ],
        compiler_params=params(),
        cost_estimate=pl.CostEstimate(
            flops=count * 2 * span * span * 1200, bytes_accessed=rows * 128 * 30, transcendentals=0
        ),
        name="scan_backward",
    )(
        stream, stream, edge, step, taps, bias, step_bias, rate, skip, mixed, grad, reach, states,
        states, carried, arriving,
    )


def parts_kernel(
    gate_ref, rest_ref, weights_ref, hidden_ref, scale_ref, gain_ref, tail_ref, next_ref, taps_ref,
    parts_out, dots_out, sums_out,
    left, edge,
):
    @pl.when(pl.program_id(0) == 0)
    def _():
        sums_out[...] = jnp.zeros_like(sums_out)

    block = left.shape[0]
    left[:, 0:128] = gate_ref[...]
    left[:, 128:896] = rest_ref[...]

    @pl.when(pl.program_id(0) == pl.num_programs(0) - 1)
    def _():
        edge[0:8] = jnp.zeros_like(edge[0:8])
        edge[8:16] = next_ref[...]
        fixed = tail_ref[...]
        for tap in range(3):
            fixed = fixed + taps_ref[tap : tap + 1] * edge[3 - tap : 11 - tap]
        high = fixed.astype(bf16)
        left[block - 8 :, 128:512] = high
        left[block - 8 :, 640:896] = (fixed - high.astype(f32))[:, 128:].astype(bf16)

    groups, _, share = parts_out.shape
    total = mm(left[...], weights_ref[...]).astype(bf16)
    scale = scale_ref[...]
    summed = None
    for at in range(0, total.shape[1], 128):
        lanes = slice(at, at + 128)
        product = total[:, lanes].astype(f32) * (hidden_ref[:, lanes].astype(f32) * scale)
        sums_out[0:1, lanes] += jnp.sum(product, axis=0, keepdims=True)
        product = product * gain_ref[:, lanes]
        summed = product if summed is None else summed + product
    dots_out[...] = jnp.sum(summed.T, axis=0, keepdims=True)
    for group in range(groups):
        parts_out[group] = total[:, group * share : (group + 1) * share]


def input_parts(
    gate16, rest16, weights, hidden_in, scale, gain, tail, next_head, taps, groups
):
    rows, width = hidden_in.shape
    block = 512
    row = lambda i: (i, 0)
    share = width // groups
    return pl.pallas_call(
        parts_kernel,
        grid=(rows // block,),
        in_specs=[
            spec((block, 128), row), spec((block, 768), row), whole_block(weights),
            spec((block, width), row), spec((block, 128), row), whole_block(gain),
            whole_block(tail), whole_block(next_head), whole_block(taps),
        ],
        out_specs=[
            spec((groups, block, share), lambda i: (0, i, 0)), spec((1, block), lambda i: (0, i)),
            spec((1, width), lambda i: (0, 0)),
        ],
        out_shape=[
            jax.ShapeDtypeStruct((groups, rows, share), bf16),
            jax.ShapeDtypeStruct((1, rows), f32),
            jax.ShapeDtypeStruct((1, width), f32),
        ],
        scratch_shapes=[pltpu.VMEM((block, 896), bf16), pltpu.VMEM((16, 384), f32)],
        compiler_params=params(),
        cost_estimate=pl.CostEstimate(
            flops=2 * rows * width * 896, bytes_accessed=rows * width * 5, transcendentals=0
        ),
        name="input_parts",
    )(gate16, rest16, weights, hidden_in, scale, gain, tail, next_head, taps)


def output_kernel(rows_ref, weights_ref, hidden_ref, parts_out):
    groups, _, share = parts_out.shape
    total = hidden_ref[...].astype(f32)
    summed = None
    for group in range(groups):
        term = mm(rows_ref[group], weights_ref[group]).astype(bf16).astype(f32)
        summed = term if summed is None else summed + term
    total = (total + summed).astype(bf16)
    for group in range(groups):
        parts_out[group] = total[:, group * share : (group + 1) * share]


def output_rows(rows, weights, hidden):
    groups, tokens, inner = rows.shape
    width = hidden.shape[1]
    block = 128
    share = width // groups
    return pl.pallas_call(
        output_kernel,
        grid=(tokens // block,),
        in_specs=[
            spec((groups, block, inner), lambda i: (0, i, 0)), whole_block(weights),
            spec((block, width), lambda i: (i, 0)),
        ],
        out_specs=spec((groups, block, share), lambda i: (0, i, 0)),
        out_shape=jax.ShapeDtypeStruct((groups, tokens, share), bf16),
        compiler_params=params(),
        cost_estimate=pl.CostEstimate(
            flops=2 * tokens * groups * inner * width, bytes_accessed=8 << 20, transcendentals=0
        ),
        name="output_rows",
    )(rows, weights, hidden)


def passed_along(block, axis, distance):
    devices = range(lax.axis_size(axis))
    route = [(i - distance, i) for i in devices if i - distance in devices]
    return lax.ppermute(block, axis, route)


def bits_of(axis):
    count = lax.axis_size(axis)
    assert count & (count - 1) == 0
    return [1 << n for n in range(count.bit_length() - 1)]


def summed_over(value, axis, turned=False):
    count = lax.axis_size(axis)
    bits = bits_of(axis)
    for bit in reversed(bits) if turned else bits:
        value = value + lax.ppermute(value, axis, [(i, i ^ bit) for i in range(count)])
    return value


def scattered_sum(value, axis):
    count = lax.axis_size(axis)
    bits = bits_of(axis)
    mine = lax.axis_index(axis)
    value = value.reshape([2] * len(bits) + [value.shape[0] // count] + list(value.shape[1:]))
    for place, bit in enumerate(bits):
        at = len(bits) - 1 - place
        own = (mine // bit) % 2
        kept = lax.dynamic_index_in_dim(value, own, at, False)
        sent = lax.dynamic_index_in_dim(value, 1 - own, at, False)
        value = kept + lax.ppermute(sent, axis, [(i, i ^ bit) for i in range(count)])
    return value


def chained(states, decays, mine, backward):
    count = states.shape[0]
    order = range(count)
    if backward:
        order = reversed(order)
    total = jnp.zeros_like(states[0])
    for at in order:
        use = at > mine if backward else at < mine
        total = jnp.where(use, decays[at][:, None] * total + states[at], total)
    return total


def block(
    hidden_in, norm_gain, gate_proj, value_proj, state_proj, step_proj, conv_value,
    conv_value_bias, conv_state, conv_state_bias, step_bias, decay_rate, skip_gain, mix_gain,
    out_proj, out_grad,
):
    rows, width = hidden_in.shape
    groups = lax.axis_size("head")
    share = width // groups
    mine = lax.axis_index("head")
    first_col = mine * share
    inner_local = gate_proj.shape[1]
    inner_width = inner_local * groups
    heads = step_proj.shape[1]
    head_size = inner_local // heads

    def wide(x):
        return jnp.repeat(x, head_size, axis=-1)

    step_wide = wide(step_proj)
    rate, skip, step_shift = (wide(x)[None, :] for x in (decay_rate, skip_gain, step_bias))
    taps = jnp.concatenate([conv_value, conv_state], axis=1)
    bias = jnp.concatenate([conv_value_bias, conv_state_bias])[None, :]
    gain = mix_gain[None, :]

    all_out_proj = lax.all_gather(out_proj, "head")
    projected, gate_in, stream, step, scale_in = project(
        hidden_in, norm_gain, gate_proj, value_proj, state_proj, step_wide
    )
    edge = passed_along(stream[rows - 8 :], "seq", 1)
    grad_gated = lax.dot_general(
        out_grad, out_proj, (((1,), (1,)), ((), ())), preferred_element_type=f32
    )
    partial_mixed, queries, reach, states = scan_forward(
        stream, edge, step, taps, bias, step_shift, rate, skip
    )
    place = lax.axis_index("seq")
    decay_here = jnp.exp(reach[rows - 1])
    packed = jnp.concatenate([states[-1], jnp.broadcast_to(decay_here[None, :], (8, 128))])
    gathered = lax.all_gather(packed, "seq")
    decays = gathered[:, 128]
    carried = chained(gathered[:, :128], decays, place, False)
    mixed, sums = join(partial_mixed, queries, reach, gate_in, grad_gated, carried, gain)
    sums = summed_over(sums, "head")
    gated_rows, grad_gate16, grad_mixed, grad_mix_gain, incoming = gate_step(
        mixed, queries, reach, gate_in, grad_gated, sums, gain, inner_width
    )

    own_tokens = rows // groups
    group_rows = lax.all_to_all(
        gated_rows.reshape(groups, own_tokens, inner_local), "head", 0, 0, tiled=False
    )
    hidden_rows = lax.dynamic_slice_in_dim(hidden_in, mine * own_tokens, own_tokens, 0)
    out_parts = output_rows(group_rows, all_out_proj, hidden_rows)
    block_out = lax.all_to_all(out_parts, "head", 0, 0, tiled=False).reshape(rows, share)

    arriving = chained(lax.all_gather(incoming, "seq"), decays, place, True)
    rest16, tail, head, sums = scan_backward(
        stream, edge, step, taps, bias, step_shift, rate, skip, mixed, grad_mixed, reach,
        states, carried, arriving,
    )
    next_head = passed_along(head, "seq", -1)
    step_back = wide(step_proj).T * (1.0 / head_size)
    weights = jnp.concatenate(
        [gate_proj.T, value_proj.T, state_proj.T, step_back.astype(bf16), state_proj.T], axis=0
    )
    parts, dots, norm_sums = input_parts(
        grad_gate16, rest16, weights, hidden_in, scale_in, norm_gain[None, :], tail, next_head,
        taps, groups,
    )
    grad_projected = lax.psum_scatter(parts, "head", scatter_dimension=0, tiled=False).astype(f32)

    rest16, next_head, projected, _ = lax.optimization_barrier(
        (rest16, next_head, projected, parts)
    )
    extra = [sum(taps[tap] * next_head[row - tap] for tap in range(row + 1)) for row in range(3)]
    tail = tail.at[5:].add(jnp.stack(extra))
    tail16 = tail.astype(bf16)
    rest16 = lax.dynamic_update_slice(rest16, tail16, (rows - 8, 0))
    low16 = (tail - tail16.astype(f32))[:, inner_local:].astype(bf16)
    rest16 = lax.dynamic_update_slice(rest16, low16, (rows - 8, 512))
    grad_gate_proj = lax.dot_general(
        projected, grad_gate16, (((0,), (0,)), ((), ())), preferred_element_type=f32
    )
    gated_rows, _ = lax.optimization_barrier((gated_rows, parts))
    grad_out_proj = lax.dot_general(
        gated_rows, out_grad, (((0,), (0,)), ((), ())), preferred_element_type=f32
    )
    grad_rest = lax.dot_general(
        projected, rest16, (((0,), (0,)), ((), ())), preferred_element_type=f32
    )
    grad_gate_proj = summed_over(grad_gate_proj, "seq")
    grad_out_proj = summed_over(grad_out_proj, "seq", True)
    grad_value_proj = summed_over(grad_rest[:, :128], "seq")
    grad_state_proj = scattered_sum(grad_rest[:, 128:384] + grad_rest[:, 512:768], "head")
    grad_state_proj = summed_over(grad_state_proj, "seq", True)
    grad_step_proj = summed_over(grad_rest[:, 384:512:head_size].T, "seq", True).T

    sums = sums.at[5, :128].set(grad_mix_gain[0])
    small = summed_over(
        jnp.concatenate([sums.reshape(-1), norm_sums.reshape(-1)]).reshape(-1, 128), "seq"
    )
    total = summed_over(jnp.concatenate([small, dots.reshape(-1, 128)]), "head").reshape(-1)
    small = small.reshape(-1)
    sums = small[: 8 * 512].reshape(8, 512)
    state_sums = total[: 8 * 512].reshape(8, 512)[:, 128:384]
    grad_norm_gain = lax.dynamic_slice_in_dim(total, 8 * 512 + first_col, share, 0)
    unit_dot = total[8 * 512 + width :]

    hidden_own = lax.dynamic_slice_in_dim(hidden_in, first_col, share, 1).astype(f32)
    gain_own = lax.dynamic_slice_in_dim(norm_gain, first_col, share, 0)
    scale_col = scale_in[:, :1]
    normal_own = hidden_own * scale_col
    grad_unit = grad_projected * gain_own[None, :]
    grad_input = scale_col * (grad_unit - normal_own * (unit_dot / width)[:, None])
    grad_input = grad_input + lax.dynamic_slice_in_dim(out_grad, first_col, share, 1).astype(f32)

    head_rows = sums[:3, 384:512].reshape(3, heads, head_size)
    return (
        block_out,
        grad_input,
        grad_norm_gain,
        grad_gate_proj,
        grad_value_proj,
        grad_state_proj,
        grad_step_proj,
        sums[:4, :128],
        sums[4, :128],
        state_sums[:4],
        state_sums[4],
        head_rows[0, :, 0],
        head_rows[1, :, 0],
        jnp.sum(head_rows[2], axis=1),
        sums[5, :128],
        grad_out_proj,
    )


def solution(mesh):
    in_specs = (
        P("seq", None), P(), P(None, "head"), P(None, "head"), P(), P(None, "head"),
        P(None, "head"), P("head"), P(), P(), P("head"), P("head"), P("head"), P("head"),
        P("head", None), P("seq", None),
    )
    out_specs = (
        P("seq", "head"), P("seq", "head"), P("head"), P(None, "head"), P(None, "head"),
        P("head", None), P(None, "head"), P(None, "head"), P("head"), P(), P(), P("head"),
        P("head"), P("head"), P("head"), P("head", None),
    )
    return jax.shard_map(block, mesh=mesh, in_specs=in_specs, out_specs=out_specs, check_vma=False)
```

```python
from functools import partial

import jax
import jax.numpy as jnp
from jax import lax
from jax.experimental import pallas as pl
from jax.experimental.pallas import tpu as pltpu
from jax.experimental.layout import Layout, with_layout_constraint
from jax.sharding import PartitionSpec as P


SPAN = 256
epsilon = 1e-05
f32 = jnp.float32
bf16 = jnp.bfloat16


def mm(a, b):
    return jnp.dot(a, b, preferred_element_type=f32)


def mm_nt(a, b):
    return lax.dot_general(a, b, (((1,), (1,)), ((), ())), preferred_element_type=f32)


def mm_tn(a, b):
    return lax.dot_general(a, b, (((0,), (0,)), ((), ())), preferred_element_type=f32)


def halves(x):
    high = x.astype(bf16)
    return jnp.concatenate([high, (x - high.astype(f32)).astype(bf16)], axis=1)


def two(x):
    high = x.astype(bf16)
    return high, (x - high.astype(f32)).astype(bf16)


def left_terms(x, axis):
    high, low = two(x)
    return jnp.concatenate([high, high, low], axis=axis)


def right_terms(x):
    high, low = two(x)
    return jnp.concatenate([high, low, high], axis=0)


def wide_terms(x):
    high, low = two(x)
    return jnp.concatenate([high, low, high], axis=1)


def folded(x):
    width = x.shape[1] // 2
    return x[:, :width] + x[:, width:]


def logistic(x):
    return 0.5 + 0.5 * jnp.tanh(0.5 * x)


def softplus(x):
    return jnp.maximum(x, 0.0) + jnp.log1p(jnp.exp(-jnp.abs(x)))


def iota(shape, axis):
    return lax.broadcasted_iota(jnp.int32, shape, axis)


def params(mebibytes):
    return pltpu.CompilerParams(
        dimension_semantics=("arbitrary",), vmem_limit_bytes=mebibytes << 20
    )


def spec(shape, index):
    return pl.BlockSpec(shape, index)


def whole_block(array):
    rank = array.ndim
    return pl.BlockSpec(array.shape, lambda *i: (0,) * rank)


def project_kernel(
    hidden_ref, gain_ref, gate_ref, value_ref, state_ref, step_ref,
    projected_ref, gate_out, stream_out, step_out, scale_out, weights,
):
    @pl.when(pl.program_id(0) == 0)
    def _():
        weights[:, 0:128] = gate_ref[...]
        weights[:, 128:256] = value_ref[...]
        weights[:, 256:512] = state_ref[...]
        weights[:, 512:640] = step_ref[...]

    hidden = hidden_ref[...].astype(f32)
    scale = lax.rsqrt(jnp.mean(hidden * hidden, axis=1, keepdims=True) + epsilon)
    projected = (hidden * scale * gain_ref[...]).astype(bf16)
    projected_ref[...] = projected
    scale_out[...] = jnp.broadcast_to(scale, scale_out.shape)
    result = mm(projected, weights[...])
    gate_out[...] = result[:, 0:128]
    stream_out[...] = result[:, 128:512].astype(bf16)
    step_out[...] = result[:, 512:640]


def project(hidden_in, norm_gain, gate_proj, value_proj, state_proj, step_wide):
    rows, width = hidden_in.shape
    span = 512
    row = lambda i: (i, 0)
    gain = norm_gain[None, :]
    return pl.pallas_call(
        project_kernel,
        grid=(rows // span,),
        in_specs=[
            spec((span, width), row), whole_block(gain), whole_block(gate_proj),
            whole_block(value_proj), whole_block(state_proj), whole_block(step_wide),
        ],
        out_specs=[
            spec((span, width), row), spec((span, 128), row), spec((span, 384), row),
            spec((span, 128), row), spec((span, 128), row),
        ],
        out_shape=[
            jax.ShapeDtypeStruct((rows, width), bf16),
            jax.ShapeDtypeStruct((rows, 128), f32),
            jax.ShapeDtypeStruct((rows, 384), bf16),
            jax.ShapeDtypeStruct((rows, 128), f32),
            jax.ShapeDtypeStruct((rows, 128), f32),
        ],
        scratch_shapes=[pltpu.VMEM((width, 640), bf16)],
        compiler_params=params(56),
        cost_estimate=pl.CostEstimate(
            flops=2 * rows * width * 640, bytes_accessed=rows * width * 4, transcendentals=0
        ),
        name="project",
    )(hidden_in, gain, gate_proj, value_proj, state_proj, step_wide)


def convolved(ext, taps, bias):
    span = SPAN
    total = bias + taps[0:1] * ext[5 : 5 + span]
    for tap in range(1, 4):
        total = total + taps[tap : tap + 1] * ext[5 + tap : 5 + tap + span]
    return total


def running_sums(log_decay):
    span = log_decay.shape[0]
    lower = (iota((span, span), 0) >= iota((span, span), 1)).astype(bf16)
    return folded(mm(lower, halves(log_decay)))


def decay_matrix(running, running_rows, head):
    span = running.shape[0]
    at = 64 * head
    spread = running[:, at : at + 1] - running_rows[at : at + 1, :]
    return jnp.exp(jnp.where(iota((span, span), 0) >= iota((span, span), 1), spread, -jnp.inf))


def forward_kernel(
    stream_ref, edge_ref, step_ref, taps_ref, bias_ref, step_bias_ref, rate_ref, skip_ref,
    mixed_out, active_out, slope_out, reach_out, steps_out, states_out,
    ext, state, offset,
):
    span = SPAN
    first = pl.program_id(0) == 0

    @pl.when(first)
    def _():
        ext[0:8] = edge_ref[...].astype(f32)
        state[...] = jnp.zeros_like(state)
        offset[...] = jnp.zeros_like(offset)

    ext[8 : 8 + span] = stream_ref[...].astype(f32)
    conv = convolved(ext, taps_ref[...], bias_ref[...])
    ext[0:8] = ext[span : span + 8]
    chance = logistic(conv)
    active = conv * chance
    active_out[...] = active
    slope_out[...] = chance * (1.0 + conv * (1.0 - chance))
    values = active[:, 0:128]
    keys = active[:, 128:256]
    queries = active[:, 256:384]
    step = step_ref[...] + step_bias_ref[...]
    widths = softplus(step)
    running = running_sums(-rate_ref[...] * widths)
    steps_out[:, 0:128] = widths
    steps_out[:, 128:256] = running
    steps_out[:, 256:384] = logistic(step)
    running_rows = running.T
    last = running[span - 1 : span, :]
    fed = widths * values
    fed16 = fed.astype(bf16)
    query_terms = left_terms(queries, 1)
    scores = mm_nt(queries.astype(bf16), keys.astype(bf16))
    low = iota((span, 128), 1) < 64
    heads = [
        mm((scores * decay_matrix(running, running_rows, head)).astype(bf16), fed16)
        for head in range(2)
    ]
    before = state[...]
    mixed = jnp.where(low, heads[0], heads[1])
    mixed = mixed + jnp.exp(running) * mm_nt(query_terms, wide_terms(before))
    mixed_out[...] = mixed + skip_ref[...] * values
    reach_out[...] = running + offset[0:1]
    offset[...] = offset[...] + last
    tails = left_terms(jnp.exp(last - running) * fed, 0)
    after = jnp.exp(running_rows[:, span - 1 : span]) * before + mm_tn(tails, right_terms(keys))
    state[...] = after
    states_out[0] = after


def scan_forward(stream, edge, step, taps, bias, step_bias, rate, skip):
    rows = stream.shape[0]
    span = SPAN
    count = rows // span
    row = lambda i: (i, 0)
    narrow, full = spec((span, 128), row), spec((span, 384), row)
    return pl.pallas_call(
        forward_kernel,
        grid=(count,),
        in_specs=[
            full, whole_block(edge), narrow, whole_block(taps), whole_block(bias),
            whole_block(step_bias), whole_block(rate), whole_block(skip),
        ],
        out_specs=[
            narrow, full, full, narrow, full, spec((1, 128, 128), lambda i: (i, 0, 0)),
        ],
        out_shape=[
            jax.ShapeDtypeStruct((rows, 128), f32),
            jax.ShapeDtypeStruct((rows, 384), f32),
            jax.ShapeDtypeStruct((rows, 384), f32),
            jax.ShapeDtypeStruct((rows, 128), f32),
            jax.ShapeDtypeStruct((rows, 384), f32),
            jax.ShapeDtypeStruct((count, 128, 128), f32),
        ],
        scratch_shapes=[
            pltpu.VMEM((span + 8, 384), f32), pltpu.VMEM((128, 128), f32), pltpu.VMEM((8, 128), f32),
        ],
        compiler_params=params(56),
        cost_estimate=pl.CostEstimate(
            flops=count * 2 * span * span * 900, bytes_accessed=rows * 128 * 50, transcendentals=0
        ),
        name="scan_forward",
    )(stream, edge, step, taps, bias, step_bias, rate, skip)


def join_kernel(
    mixed_ref, query_ref, reach_ref, gate_ref, grad_ref, carried_ref, gain_ref, mixed_out, sums_out
):
    inner = mm_nt(left_terms(query_ref[...], 1), wide_terms(carried_ref[...]))
    mixed = mixed_ref[...] + jnp.exp(reach_ref[...]) * inner
    mixed_out[...] = mixed
    gate = gate_ref[...]
    gated = mixed * (gate * logistic(gate))
    at = 2 * pl.program_id(0)
    sums_out[pl.ds(at, 1), :] = jnp.sum((gated * gated).T, axis=0, keepdims=True)
    product = grad_ref[...] * gain_ref[...] * gated
    sums_out[pl.ds(at + 1, 1), :] = jnp.sum(product.T, axis=0, keepdims=True)


def join(mixed, active, reach, gate, grad, carried, gain):
    rows = mixed.shape[0]
    block = 1024
    sums = (2 * rows // block, block)
    blocks = spec((block, 128), lambda i: (i, 0))
    return pl.pallas_call(
        join_kernel,
        grid=(rows // block,),
        in_specs=[
            blocks, spec((block, 128), lambda i: (i, 2)), blocks, blocks, blocks,
            whole_block(carried), whole_block(gain),
        ],
        out_specs=[blocks, spec(sums, lambda i: (0, 0))],
        out_shape=[jax.ShapeDtypeStruct((rows, 128), f32), jax.ShapeDtypeStruct(sums, f32)],
        compiler_params=params(56),
        cost_estimate=pl.CostEstimate(
            flops=2 * rows * 128 * 128, bytes_accessed=rows * 128 * 22, transcendentals=0
        ),
        name="join",
    )(mixed, active, reach, gate, grad, carried, gain)


def gate_kernel(
    inner_width,
    mixed_ref, query_ref, reach_ref, gate_ref, grad_ref, sums_ref, gain_ref,
    rows_out, gate_out, mixed_grad_out, gain_out, incoming_out,
):
    @pl.when(pl.program_id(0) == 0)
    def _():
        gain_out[...] = jnp.zeros_like(gain_out)
        incoming_out[...] = jnp.zeros_like(incoming_out)

    block = mixed_ref.shape[0]
    at = 2 * pl.program_id(0)
    square = jnp.broadcast_to(sums_ref[pl.ds(at, 1), :], (128, block)).T
    product = jnp.broadcast_to(sums_ref[pl.ds(at + 1, 1), :], (128, block)).T
    scale = lax.rsqrt(square / inner_width + epsilon)
    gate = gate_ref[...]
    chance = logistic(gate)
    act = gate * chance
    mixed = mixed_ref[...]
    hat = mixed * act * scale
    rows_out[...] = (hat * gain_ref[...]).astype(bf16)
    grad = grad_ref[...]
    gain_out[...] += jnp.sum(grad * hat, axis=0, keepdims=True)
    pre = scale * (grad * gain_ref[...] - hat * (product * scale / inner_width))
    mixed_grad = pre * act
    mixed_grad_out[...] = mixed_grad
    gate_out[...] = (pre * mixed * (chance * (1.0 + gate * (1.0 - chance)))).astype(bf16)
    incoming_out[...] += mm_tn(
        left_terms(jnp.exp(reach_ref[...]) * mixed_grad, 0), right_terms(query_ref[...])
    )


def gate_step(mixed, active, reach, gate, grad, sums, gain, inner_width):
    rows = mixed.shape[0]
    block = sums.shape[1]
    blocks = spec((block, 128), lambda i: (i, 0))
    return pl.pallas_call(
        partial(gate_kernel, inner_width),
        grid=(rows // block,),
        in_specs=[
            blocks, spec((block, 128), lambda i: (i, 2)), blocks, blocks, blocks, whole_block(sums),
            whole_block(gain),
        ],
        out_specs=[
            blocks, blocks, blocks, spec((1, 128), lambda i: (0, 0)),
            spec((128, 128), lambda i: (0, 0)),
        ],
        out_shape=[
            jax.ShapeDtypeStruct((rows, 128), bf16),
            jax.ShapeDtypeStruct((rows, 128), bf16),
            jax.ShapeDtypeStruct((rows, 128), f32),
            jax.ShapeDtypeStruct((1, 128), f32),
            jax.ShapeDtypeStruct((128, 128), f32),
        ],
        compiler_params=params(56),
        cost_estimate=pl.CostEstimate(
            flops=2 * rows * 128 * 128, bytes_accessed=rows * 128 * 26, transcendentals=0
        ),
        name="gate_step",
    )(mixed, active, reach, gate, grad, sums, gain)


def head_sums(x):
    same = (iota((128, 128), 0) < 64) == (iota((128, 128), 1) < 64)
    ones = same.astype(bf16)
    high = x.astype(bf16)
    return mm(high, ones) + mm((x - high.astype(f32)).astype(bf16), ones)


def backward_kernel(
    first_chunk,
    stream_ref, before_ref, edge_ref, active_ref, slope_ref, steps_ref, taps_ref, rate_ref, skip_ref,
    mixed_ref, grad_ref, reach_ref, start_ref, end_ref, carried_ref, arriving_ref, next_ref,
    stream_grad_out, tail_out, head_out, sums_out, leaving_out,
    ext, grads, state_grad,
):
    span = SPAN
    chunk = first_chunk - pl.program_id(0)

    @pl.when(pl.program_id(0) == 0)
    def _():
        state_grad[...] = arriving_ref[...]
        grads[span : span + 8] = next_ref[...]
        sums_out[...] = jnp.zeros_like(sums_out)

    @pl.when(chunk == 0)
    def _():
        ext[0:8] = edge_ref[...].astype(f32)

    @pl.when(chunk > 0)
    def _():
        ext[0:8] = before_ref[8:16].astype(f32)

    ext[8 : 8 + span] = stream_ref[...].astype(f32)
    taps = taps_ref[...]
    values = active_ref[:, 0:128]
    keys = active_ref[:, 128:256]
    queries = active_ref[:, 256:384]
    keys16 = keys.astype(bf16)
    rate = rate_ref[...]
    widths = steps_ref[:, 0:128]
    running = steps_ref[:, 128:256]
    running_rows = running.T
    last = running[span - 1 : span, :]
    fed = widths * values
    fed16 = fed.astype(bf16)
    grad = grad_ref[...]
    grad16 = grad.astype(bf16)
    scores = mm_nt(queries.astype(bf16), keys16)
    low = iota((span, 128), 1) < 64
    grad_turned = pltpu.roll(grad, 64, 1)
    fed_turned = pltpu.roll(fed, 64, 1)
    score_grad = None
    fed_grads = []
    for head in range(2):
        decay = decay_matrix(running, running_rows, head)
        mine = low == (head == 0)
        grad_high, grad_low = two(jnp.where(mine, grad, grad_turned))
        left = [jnp.where(low, grad_high, grad_low), jnp.where(low, grad_high, 0)]
        right = two(jnp.where(mine, fed, fed_turned))
        part = mm_nt(jnp.concatenate(left, axis=1), jnp.concatenate(right, axis=1)) * decay
        score_grad = part if score_grad is None else score_grad + part
        fed_grads.append(mm_tn((scores * decay).astype(bf16), grad16))

    offset = (reach_ref[span - 8 : span, :] - running[span - 8 : span, :]).T[:, 7:8]
    carried = jnp.exp(offset) * carried_ref[...]
    before = jnp.where(chunk > 0, start_ref[0], 0.0) + carried
    last_rows = jnp.exp(running_rows[:, span - 1 : span])
    after = end_ref[0] + last_rows * carried
    after_grad = state_grad[...]
    tail = jnp.exp(last - running)
    reached = jnp.exp(running) * grad
    query_terms = right_terms(queries)
    fed_grad = jnp.where(low, fed_grads[0], fed_grads[1])
    fed_grad = fed_grad + tail * mm_nt(keys16, after_grad.astype(bf16))
    score_high, score_low = two(score_grad)
    query_grad = mm(
        jnp.concatenate([score_high, score_high, score_low], axis=1), right_terms(keys)
    ) + mm(left_terms(reached, 1), right_terms(before))
    key_grad = mm_tn(
        jnp.concatenate([score_high, score_high, score_low], axis=0), query_terms
    ) + mm(left_terms(tail * fed, 1), right_terms(after_grad))
    leaving = last_rows * after_grad + mm_tn(left_terms(reached, 0), query_terms)
    state_grad[...] = leaving
    leaving_out[...] = leaving
    value_grad = widths * fed_grad + skip_ref[...] * grad

    mixed = mixed_ref[...] - skip_ref[...] * values
    balance = head_sums(grad16.astype(f32) * mixed - fed16.astype(f32) * fed_grad)
    upper = (iota((span, span), 0) <= iota((span, span), 1)).astype(bf16)
    boundary = head_sums(
        jnp.broadcast_to(jnp.sum((after_grad * after).T, axis=0, keepdims=True), (8, 128))
    )
    decay_grad = folded(mm(upper, halves(balance))) + boundary[0:1]
    width_grad = head_sums(values * fed_grad) - rate * decay_grad
    step_grad = width_grad * steps_ref[:, 256:384]
    sums_out[0:1, 384:512] += jnp.sum(step_grad, axis=0, keepdims=True)
    sums_out[1:2, 384:512] += jnp.sum(-widths * decay_grad, axis=0, keepdims=True)
    sums_out[2:3, 384:512] += jnp.sum(grad * values, axis=0, keepdims=True)

    conv_grad = jnp.concatenate([value_grad, key_grad, query_grad], axis=1) * slope_ref[...]
    grads[0:span] = conv_grad
    for tap in range(4):
        sums_out[tap : tap + 1, 0:384] += jnp.sum(
            conv_grad * ext[5 + tap : 5 + tap + span], axis=0, keepdims=True
        )
    sums_out[4:5, 0:384] += jnp.sum(conv_grad, axis=0, keepdims=True)
    stream_grad = taps[3:4] * conv_grad
    for tap in range(3):
        stream_grad = stream_grad + taps[tap : tap + 1] * grads[3 - tap : 3 - tap + span]
    high = stream_grad.astype(bf16)
    stream_grad_out[:, 0:384] = high
    stream_grad_out[:, 384:512] = step_grad.astype(bf16)
    stream_grad_out[:, 512:768] = (stream_grad - high.astype(f32))[:, 128:384].astype(bf16)

    @pl.when(pl.program_id(0) == 0)
    def _():
        tail_out[...] = stream_grad[span - 8 :]

    head_out[...] = conv_grad[0:8]
    grads[span : span + 8] = conv_grad[0:8]


def scan_backward(
    late, stream, edge, active, slope, steps, taps, rate, skip, mixed, grad, reach, states, carried,
    arriving, next_rows,
):
    rows = stream.shape[0]
    span = SPAN
    count = rows // span // 2
    first = 2 * count - 1 if late else count - 1
    row = lambda i: (first - i, 0)
    fixed = lambda i: (0, 0)
    narrow, full = spec((span, 128), row), spec((span, 384), row)
    return pl.pallas_call(
        partial(backward_kernel, first),
        grid=(count,),
        in_specs=[
            full, spec((16, 384), lambda i: (jnp.maximum((first - i) * (span // 16) - 1, 0), 0)),
            whole_block(edge), full, full, full, whole_block(taps), whole_block(rate),
            whole_block(skip), narrow, narrow, narrow,
            spec((1, 128, 128), lambda i: (jnp.maximum(first - 1 - i, 0), 0, 0)),
            spec((1, 128, 128), lambda i: (first - i, 0, 0)),
            whole_block(carried), whole_block(arriving), whole_block(next_rows),
        ],
        out_specs=[
            spec((span, 768), lambda i: (count - 1 - i, 0)), spec((8, 384), fixed),
            spec((8, 384), fixed), spec((8, 512), fixed), spec((128, 128), fixed),
        ],
        out_shape=[
            jax.ShapeDtypeStruct((rows // 2, 768), bf16),
            jax.ShapeDtypeStruct((8, 384), f32),
            jax.ShapeDtypeStruct((8, 384), f32),
            jax.ShapeDtypeStruct((8, 512), f32),
            jax.ShapeDtypeStruct((128, 128), f32),
        ],
        scratch_shapes=[
            pltpu.VMEM((span + 8, 384), f32), pltpu.VMEM((span + 8, 384), f32),
            pltpu.VMEM((128, 128), f32),
        ],
        compiler_params=params(56),
        cost_estimate=pl.CostEstimate(
            flops=count * 2 * span * span * 1500, bytes_accessed=rows * 128 * 30, transcendentals=0
        ),
        name="scan_backward",
    )(
        stream, stream, edge, active, slope, steps, taps, rate, skip, mixed, grad, reach, states,
        states, carried, arriving, next_rows,
    )


def group_of(rows, index):
    half = rows // SPAN // 2
    if index == 0:
        return half // 2 - 1, lambda place: half + place
    return half // 2 + 1, lambda place: jnp.where(place < half, place, place + half - 2)


def parts_kernel(
    block_of, count, last_block, early_blocks,
    half_ref, gate_ref, early_ref, late_ref, weights_ref, hidden_ref, scale_ref, gain_ref, tail_ref,
    next_ref, taps_ref,
    parts_out, dots_out, sums_out,
    left, edge,
):
    at_block = block_of(half_ref[0] * count + pl.program_id(0))

    @pl.when(pl.program_id(0) == 0)
    def _():
        sums_out[...] = jnp.zeros_like(sums_out)

    block = left.shape[0]
    left[:, 0:128] = gate_ref[...]

    @pl.when(at_block < early_blocks)
    def _():
        left[:, 128:640] = early_ref[...]

    @pl.when(at_block >= early_blocks)
    def _():
        left[:, 128:640] = late_ref[...]

    @pl.when(at_block == last_block)
    def _():
        edge[0:8] = jnp.zeros_like(edge[0:8])
        edge[8:16] = next_ref[...]
        fixed = tail_ref[...]
        for tap in range(3):
            fixed = fixed + taps_ref[tap : tap + 1] * edge[3 - tap : 11 - tap]
        left[block - 8 :, 128:512] = fixed.astype(bf16)

    chips, _, share = parts_out.shape
    total = mm(left[...], weights_ref[...]).astype(bf16)
    scale = scale_ref[...]
    summed = None
    for at in range(0, total.shape[1], 128):
        lanes = slice(at, at + 128)
        product = total[:, lanes].astype(f32) * (hidden_ref[:, lanes].astype(f32) * scale)
        sums_out[0:1, lanes] += jnp.sum(product, axis=0, keepdims=True)
        product = product * gain_ref[:, lanes]
        summed = product if summed is None else summed + product
    dots_out[...] = jnp.sum(summed.T, axis=0, keepdims=True)
    for chip in range(chips):
        parts_out[chip] = total[:, chip * share : (chip + 1) * share]


def input_parts(
    index, half, gate16, early16, late16, weights, hidden_in, scale, gain, tail, next_head, taps, chips
):
    rows, width = hidden_in.shape
    block = SPAN
    count, block_of = group_of(rows, index)
    blocks = rows // block
    at = lambda i, half: block_of(half[0] * count + i)
    row = lambda i, half: (at(i, half), 0)
    share = width // chips
    return pl.pallas_call(
        partial(parts_kernel, block_of, count, blocks - 1, blocks // 2),
        grid_spec=pltpu.PrefetchScalarGridSpec(
            num_scalar_prefetch=1,
            grid=(count,),
            in_specs=[
                spec((block, 128), row),
                spec((block, 512), lambda i, half: (jnp.minimum(at(i, half), blocks // 2 - 1), 0)),
                spec((block, 512), lambda i, half: (jnp.maximum(at(i, half) - blocks // 2, 0), 0)),
                whole_block(weights), spec((block, width), row), spec((block, 128), row),
                whole_block(gain), whole_block(tail), whole_block(next_head), whole_block(taps),
            ],
            out_specs=[
                spec((chips, block, share), lambda i, half: (0, i, 0)),
                spec((1, block), lambda i, half: (0, i)),
                spec((1, width), lambda i, half: (0, 0)),
            ],
            scratch_shapes=[pltpu.VMEM((block, 640), bf16), pltpu.VMEM((16, 384), f32)],
        ),
        out_shape=[
            jax.ShapeDtypeStruct((chips, count * block, share), bf16),
            jax.ShapeDtypeStruct((1, count * block), f32),
            jax.ShapeDtypeStruct((1, width), f32),
        ],
        compiler_params=params(56),
        cost_estimate=pl.CostEstimate(
            flops=2 * count * block * width * 640, bytes_accessed=count * block * width * 5,
            transcendentals=0,
        ),
        name="input_parts",
    )(
        half.astype(jnp.int32)[None], gate16, early16, late16, weights, hidden_in, scale, gain, tail,
        next_head, taps,
    )


def output_kernel(at_ref, rows_ref, weights_ref, hidden_ref, parts_out):
    chips, _, _, share = parts_out.shape
    summed = None
    for group in range(rows_ref.shape[0]):
        term = mm(rows_ref[group], weights_ref[group]).astype(bf16).astype(f32)
        summed = term if summed is None else summed + term
    total = (hidden_ref[...].astype(f32) + summed).astype(bf16)
    for chip in range(chips):
        parts_out[chip, 0] = total[:, chip * share : (chip + 1) * share]


def output_rows(rows, weights, hidden, at, chips):
    groups, tokens, inner = rows.shape
    width = hidden.shape[1]
    block = tokens // 2
    share = width // chips
    return pl.pallas_call(
        output_kernel,
        grid_spec=pltpu.PrefetchScalarGridSpec(
            num_scalar_prefetch=1,
            grid=(2,),
            in_specs=[
                spec((groups, block, inner), lambda i, at: (0, i, 0)), whole_block(weights),
                spec((block, width), lambda i, at: (2 * at[0] + i, 0)),
            ],
            out_specs=spec((chips, 1, block, share), lambda i, at: (0, i, 0, 0)),
        ),
        out_shape=jax.ShapeDtypeStruct((chips, 2, block, share), bf16),
        compiler_params=params(56),
        cost_estimate=pl.CostEstimate(
            flops=2 * tokens * groups * inner * width, bytes_accessed=8 << 20, transcendentals=0
        ),
        name="output_rows",
    )(at, rows, weights, hidden)


def row_major(x):
    return with_layout_constraint(x, Layout(major_to_minor=(0, 1)))


def passed_along(block, axis, distance):
    devices = range(lax.axis_size(axis))
    route = [(i - distance, i) for i in devices if i - distance in devices]
    return lax.ppermute(block, axis, route)


def bits_of(axis):
    count = lax.axis_size(axis)
    assert count & (count - 1) == 0
    return [1 << n for n in range(count.bit_length() - 1)]


def summed_over(value, axis, turned=False):
    count = lax.axis_size(axis)
    bits = bits_of(axis)
    for bit in reversed(bits) if turned else bits:
        value = value + lax.ppermute(value, axis, [(i, i ^ bit) for i in range(count)])
    return value


def spread_sums(pair, axis):
    chips = pair.shape[0]
    mine = lax.axis_index(axis)
    spread = jnp.stack([pair, jnp.zeros_like(pair)], axis=1)
    spread = jnp.where(mine % 2 == 0, spread, spread[:, ::-1])
    spread = spread.reshape(2 * chips, *pair.shape[1:])
    return lax.psum_scatter(spread, axis, scatter_dimension=0, tiled=False).astype(f32)


def line_kernel(at_ref, up_own, up_got, down_own, down_got, *refs):
    up_out, down_out = refs[-2:]
    up = up_own[0].astype(f32) + up_got[0].astype(f32)
    down = down_own[0].astype(f32) + down_got[0].astype(f32)
    if len(refs) == 4:
        up, down = up + refs[0][...].astype(f32), down + refs[1][...].astype(f32)
    up_out[...] = up.astype(bf16)
    down_out[...] = down.astype(bf16)


def line_step(up_at, down_at, own, got, arrived):
    chips, rows, width = own.shape
    block = rows // 2
    at = jnp.stack([up_at, down_at]).astype(jnp.int32)
    at = jnp.clip(at, 0, chips - 1)
    blocks = [spec((1, block, width), lambda i, at, k=k: (at[k], i, 0)) for k in (0, 0, 1, 1)]
    plain = spec((block, width), lambda i, at: (i, 0))
    return pl.pallas_call(
        line_kernel,
        grid_spec=pltpu.PrefetchScalarGridSpec(
            num_scalar_prefetch=1,
            grid=(rows // block,),
            in_specs=blocks + [plain] * len(arrived),
            out_specs=[plain, plain],
        ),
        out_shape=[jax.ShapeDtypeStruct((rows, width), bf16)] * 2,
        compiler_params=params(56),
        cost_estimate=pl.CostEstimate(
            flops=rows * width * 4, bytes_accessed=rows * width * 16, transcendentals=0
        ),
        name="line_step",
    )(at, own, got, own, got, *arrived)


def line_sent(step, sent, axis):
    chips, cores = 4, 2
    last = chips * cores - 1
    up = lax.ppermute(sent[0], axis, [(i, i + cores) for i in range(cores * step)])
    down_route = [(last - i, last - i - cores) for i in range(cores * step)]
    down = lax.ppermute(sent[1], axis, down_route)
    return up, down


def line_terms(step, own, got, arrived, axis):
    chip = lax.axis_index(axis) // 2
    return line_step(4 + chip - step, step - 4 + chip, own, got, arrived)


after = lax.optimization_barrier


def finish_kernel(
    width,
    place_ref, own_ref, got_ref, up_ref, down_ref, hidden_ref, scale_ref, gain_ref, dots_ref,
    grad_ref, *refs,
):
    kept_out, sent_out = refs[-2:]
    total = own_ref[0].astype(f32) + got_ref[0].astype(f32)
    total = total + up_ref[...].astype(f32) + down_ref[...].astype(f32)
    share, block = kept_out.shape
    dot = jnp.broadcast_to(dots_ref[...], (128, block)).T * (1.0 / width)
    scale = scale_ref[...]
    parts = []
    for at in range(0, total.shape[1], 128):
        lanes = slice(at, at + 128)
        normal = hidden_ref[:, lanes].astype(f32) * scale
        unit = total[:, lanes] * gain_ref[:, lanes]
        parts.append(scale * (unit - normal * dot) + grad_ref[:, lanes].astype(f32))
    result = jnp.concatenate([part.T for part in parts], axis=0)
    second = place_ref[1] == 1
    kept_out[...] = jnp.where(second, result[share:], result[:share])
    sent_out[...] = jnp.where(second, result[:share], result[share:])


def finish(
    index, own, got, up, down, hidden_in, scale, gain, dots, out_grad, place, target
):
    rows, width = hidden_in.shape
    both = own.shape[2]
    block = SPAN
    count, block_of = group_of(rows, index)
    here = lambda i, at: (at[0], i, 0)
    local_row = lambda i, at: (i, 0)
    token = lambda i, at: (block_of(at[1] * count + i), 0)
    feature = lambda i, at: (block_of(at[1] * count + i), at[0])
    share = both // 2
    operands = [place, own, got, up, down, hidden_in, scale, gain, dots, out_grad]
    in_specs = [
        spec((1, block, both), here), spec((1, block, both), here),
        spec((block, both), local_row), spec((block, both), local_row),
        spec((block, both), feature), spec((block, 128), token),
        spec((1, both), lambda i, at: (0, at[0])), spec((1, block), lambda i, at: (0, i)),
        spec((block, both), feature),
    ]
    aliases = {}
    if target is not None:
        aliases = {len(operands): 0}
        operands.append(target)
        in_specs.append(pl.BlockSpec(memory_space=pl.ANY))
    return pl.pallas_call(
        partial(finish_kernel, width),
        grid_spec=pltpu.PrefetchScalarGridSpec(
            num_scalar_prefetch=1,
            grid=(count,),
            in_specs=in_specs,
            out_specs=[
                spec((share, block), lambda i, at: (0, block_of(at[1] * count + i))),
                spec((share, block), lambda i, at: (0, i)),
            ],
        ),
        out_shape=[
            jax.ShapeDtypeStruct((share, rows), f32),
            jax.ShapeDtypeStruct((share, count * block), f32),
        ],
        input_output_aliases=aliases,
        compiler_params=params(56),
        cost_estimate=pl.CostEstimate(
            flops=rows * both * 5, bytes_accessed=count * block * both * 16, transcendentals=0
        ),
        name="finish",
    )(*operands)


def place_kernel(place_ref, received_ref, target_ref, out_ref):
    out_ref[...] = received_ref[...]


def placed(received, target, place, block_at):
    block = SPAN
    share = received.shape[0]
    return pl.pallas_call(
        place_kernel,
        grid_spec=pltpu.PrefetchScalarGridSpec(
            num_scalar_prefetch=1,
            grid=(received.shape[1] // block,),
            in_specs=[
                spec((share, block), lambda i, at: (0, i)), pl.BlockSpec(memory_space=pl.ANY),
            ],
            out_specs=spec((share, block), lambda i, at: (0, block_at(i, 1 - at[1]))),
        ),
        out_shape=jax.ShapeDtypeStruct(target.shape, target.dtype),
        input_output_aliases={2: 0},
        compiler_params=params(56),
        name="placed",
    )(place, received, target)


def split_kernel(place_ref, rows_ref, kept_out, sent_out):
    share = kept_out.shape[0]
    rows = rows_ref[...].astype(f32).T
    second = place_ref[1] == 1
    kept_out[...] = jnp.where(second, rows[share:], rows[:share]).astype(bf16)
    sent_out[...] = jnp.where(second, rows[:share], rows[share:]).astype(bf16)


def split(rows, place, block_at):
    block = SPAN
    count, both = rows.shape
    share = both // 2
    return pl.pallas_call(
        split_kernel,
        grid_spec=pltpu.PrefetchScalarGridSpec(
            num_scalar_prefetch=1,
            grid=(count // block,),
            in_specs=[spec((block, both), lambda i, at: (i, 0))],
            out_specs=[
                spec((share, block), lambda i, at: (0, block_at(i, at[1]))),
                spec((share, block), lambda i, at: (0, i)),
            ],
        ),
        out_shape=[
            jax.ShapeDtypeStruct((share, 2 * count), bf16),
            jax.ShapeDtypeStruct((share, count), bf16),
        ],
        compiler_params=params(56),
        name="split",
    )(place, rows)


def swapped(mine, other_first, axis):
    count = lax.axis_size(axis)
    share = mine.shape[-1] // 2
    low, high = mine[..., :share], mine[..., share:]
    kept = jnp.where(other_first, high, low)
    sent = jnp.where(other_first, low, high).astype(bf16)
    got = lax.ppermute(sent, axis, [(i, i ^ 1) for i in range(count)]).astype(kept.dtype)
    at = mine.ndim - 2
    return jnp.where(
        other_first, jnp.stack([got, kept], axis=at), jnp.stack([kept, got], axis=at)
    )


def chained(states, decays, mine, backward):
    count = states.shape[0]
    order = range(count)
    if backward:
        order = reversed(order)
    total = jnp.zeros_like(states[0])
    for at in order:
        use = at > mine if backward else at < mine
        total = jnp.where(use, decays[at][:, None] * total + states[at], total)
    return total


def block(
    hidden_in, norm_gain, gate_proj, value_proj, state_proj, step_proj, conv_value,
    conv_value_bias, conv_state, conv_state_bias, step_bias, decay_rate, skip_gain, mix_gain,
    out_proj, out_grad,
):
    rows, width = hidden_in.shape
    groups = lax.axis_size("head")
    share = width // groups
    mine = lax.axis_index("head")
    first_col = mine * share
    chips = groups // 2
    core = mine % 2
    second = core == 1
    inner_local = gate_proj.shape[1]
    inner_width = inner_local * groups
    heads = step_proj.shape[1]
    head_size = inner_local // heads

    def wide(x):
        return jnp.repeat(x, head_size, axis=-1)

    step_wide = wide(step_proj)
    rate, skip, step_shift = (wide(x)[None, :] for x in (decay_rate, skip_gain, step_bias))
    taps = jnp.concatenate([conv_value, conv_state], axis=1)
    bias = jnp.concatenate([conv_value_bias, conv_state_bias])[None, :]
    gain = mix_gain[None, :]

    all_out_proj = lax.all_gather(out_proj, "head")
    projected, gate_in, stream, step, scale_in = project(
        hidden_in, norm_gain, gate_proj, value_proj, state_proj, step_wide
    )
    edge = passed_along(stream[rows - 8 :], "seq", 1)
    grad_gated = lax.dot_general(
        out_grad, out_proj, (((1,), (1,)), ((), ())), preferred_element_type=f32
    )
    partial_mixed, active, slope, reach, steps, states = scan_forward(
        stream, edge, step, taps, bias, step_shift, rate, skip
    )
    at_seq = lax.axis_index("seq")
    decay_here = jnp.exp(reach[rows - 1])
    packed = jnp.concatenate([states[-1], jnp.broadcast_to(decay_here[None, :], (8, 128))])
    gathered = lax.all_gather(packed, "seq")
    decays = gathered[:, 128]
    carried = chained(gathered[:, :128], decays, at_seq, False)
    mixed, sums = join(partial_mixed, active, reach, gate_in, grad_gated, carried, gain)
    sums = summed_over(sums, "head")
    gated_rows, grad_gate16, grad_mixed, grad_mix_gain, incoming = gate_step(
        mixed, active, reach, gate_in, grad_gated, sums, gain, inner_width
    )

    own_tokens = rows // groups
    group_rows = lax.all_to_all(
        gated_rows.reshape(groups, own_tokens, inner_local), "head", 0, 0, tiled=False
    )
    on_line = chips == 4 and 2 * share % 128 == 0 and own_tokens == 2 * SPAN
    partner = [(i, i ^ 1) for i in range(groups)]
    place = jnp.stack([mine // 2, core]).astype(jnp.int32)
    arriving = chained(lax.all_gather(incoming, "seq"), decays, at_seq, True)
    scan_args = (
        stream, edge, active, slope, steps, taps, rate, skip, mixed, grad_mixed, reach, states, carried
    )
    late16, tail, head, late_sums, arriving = scan_backward(
        True, *scan_args, arriving, jnp.zeros((8, stream.shape[1]), f32)
    )
    step_back = wide(step_proj).T * (1.0 / head_size)
    weights = jnp.concatenate(
        [gate_proj.T, value_proj.T, state_proj.T, step_back.astype(bf16)], axis=0
    )
    gain_in = norm_gain[None, :]

    def parts_of(index, half, early16, next_head, weights):
        return input_parts(
            index, half, grad_gate16, early16, late16, weights, hidden_in, scale_in, gain_in, tail,
            next_head, taps, chips,
        )

    def exchanged(other):
        return lax.ppermute(other, "head", partner)

    def both_halves(own, other):
        return jnp.concatenate(
            [jnp.where(second, other, own), jnp.where(second, own, other)], axis=0
        )

    other_0, other_dots, other_sums = parts_of(0, 1 - core, late16, head, weights)
    got_0 = exchanged(other_0)
    own_0, own_dots, own_sums = parts_of(0, core, late16, head, weights)
    norm_sums, dots_0 = other_sums + own_sums, both_halves(own_dots, other_dots)
    if on_line:
        line_0 = line_sent(1, line_terms(1, own_0, got_0, (), "head"), "head")
    early16, _, head, early_sums, _ = scan_backward(False, *scan_args, arriving, head)
    next_head = passed_along(head, "seq", -1)
    if on_line:
        line_0, _ = after((line_0, early16))
        sent, group_rows = after((line_terms(2, own_0, got_0, line_0, "head"), group_rows))
        line_0 = line_sent(2, sent, "head")
    out_parts = output_rows(
        group_rows, all_out_proj, hidden_in, mine.astype(jnp.int32)[None], chips
    )
    out_parts = out_parts.reshape(groups, own_tokens // 2, 2 * share)
    out_parts = lax.all_to_all(out_parts, "head", 0, 0, tiled=False)
    other_1, other_dots, other_sums = parts_of(1, 1 - core, early16, next_head, weights)
    got_1 = exchanged(other_1)
    if on_line:
        line_0, other_dots = after((line_0, other_dots))
        sent, weights = after((line_terms(3, own_0, got_0, line_0, "head"), weights))
        line_0 = line_sent(3, sent, "head")
    own_1, own_dots, own_sums = parts_of(1, core, early16, next_head, weights)
    norm_sums, dots_1 = norm_sums + other_sums + own_sums, both_halves(own_dots, other_dots)
    dots = jnp.concatenate([dots_0.reshape(-1, 128), dots_1.reshape(-1, 128)], axis=0)
    needs = (late16, next_head, projected, gated_rows)
    if on_line:
        sent, needs, dots = after((line_terms(1, own_1, got_1, (), "head"), needs, dots))
        line_1 = line_sent(1, sent, "head")
    sums = (late_sums + early_sums).at[5, :128].set(grad_mix_gain[0])
    headed = jnp.concatenate(
        [sums[:5, 128:384].reshape(-1, 128), norm_sums.reshape(-1, 128), dots], axis=0
    )
    headed = summed_over(headed, "head", False)
    unit_dot, headed = headed[-dots.shape[0] :], headed[: -dots.shape[0]]

    def dots_of(total):
        total = total.reshape(-1)
        return total[: dots_0.size].reshape(2, -1), total[dots_0.size :].reshape(2, -1)

    late_fixed, next_rows, projected, gated_rows = needs
    extra = [sum(taps[tap] * next_rows[row - tap] for tap in range(row + 1)) for row in range(3)]
    fixed = tail.at[5:].add(jnp.stack(extra))
    fixed16 = fixed.astype(bf16)
    low16 = (fixed - fixed16.astype(f32))[:, inner_local:].astype(bf16)
    late_fixed = lax.dynamic_update_slice(late_fixed, fixed16, (rows // 2 - 8, 0))
    late_fixed = lax.dynamic_update_slice(late_fixed, low16, (rows // 2 - 8, 512))
    contract = (((0,), (0,)), ((), ()))
    rest16 = jnp.concatenate([early16, late_fixed], axis=0)

    def product(left, right):
        return lax.dot_general(left, right, contract, preferred_element_type=f32)

    grad_rest = product(projected, rest16)
    state_part = row_major(grad_rest[:, 128:384] + grad_rest[:, 512:768])
    grad_value_proj = row_major(grad_rest[:, :128])
    step_sums = row_major(grad_rest[:, 384:512]).T[::head_size]
    if on_line:
        line_1, unit_dot, state_part = after((line_1, unit_dot, state_part))
        sent = line_terms(2, own_1, got_1, line_1, "head")
        sent, gated_rows, projected, sums = after((sent, gated_rows, projected, sums))
        line_1 = line_sent(2, sent, "head")
    grad_gate_proj = row_major(product(projected, grad_gate16))
    grad_out_proj = product(gated_rows, out_grad)
    grad_state_proj = lax.psum_scatter(state_part, "head", scatter_dimension=0, tiled=True)
    grad_state_proj = summed_over(grad_state_proj, "seq", False)
    grad_value_proj, grad_gate_proj = (
        total.astype(f32)
        for total in lax.psum((grad_value_proj.astype(bf16), grad_gate_proj.astype(bf16)), "seq")
    )
    grad_out_proj = summed_over(grad_out_proj, "seq", True)

    small = jnp.concatenate(
        [sums.reshape(-1, 128), step_sums.reshape(-1, 128), headed.reshape(-1, 128)], axis=0
    )
    small = summed_over(small, "seq", False).reshape(-1)
    at = sums.size
    sums, small = small[:at].reshape(8, 512), small[at:]
    grad_step_proj, small = small[: heads * width].reshape(heads, width).T, small[heads * width :]
    state_sums, norm_sums = small[: 5 * 256].reshape(5, 256), small[5 * 256 :]
    grad_norm_gain = lax.dynamic_slice_in_dim(norm_sums, first_col, share, 0)
    if on_line:
        sent = line_terms(3, own_1, got_1, line_1, "head")
        sent, own_0, out_parts = after((sent, own_0, out_parts))
        line_1 = line_sent(3, sent, "head")
        own_block = lambda i, core: 2 * i + core
        block_out, out_sent = split(out_parts.reshape(rows // 2, 2 * share), place, own_block)
        received = lax.ppermute(out_sent, "head", partner)
        block_out = placed(received, block_out, place, own_block).T
        line_dots = dots_of(unit_dot)
        grad_input = None
        for index, own, got, (up, down), dots in (
            (0, own_0, got_0, line_0, line_dots[0]), (1, own_1, got_1, line_1, line_dots[1])
        ):
            count, block_of = group_of(rows, index)
            own_dots = jnp.where(second, dots[1:], dots[:1])
            grad_input, sent = finish(
                index, own, got, up, down, hidden_in, scale_in, gain_in, own_dots, out_grad, place,
                grad_input,
            )
            received = lax.ppermute(sent, "head", partner)
            grad_input = placed(
                received, grad_input, place,
                lambda i, core, count=count, block_of=block_of: block_of(core * count + i),
            )
        grad_input = grad_input.T
    else:
        block_out = swapped(out_parts, second, "head").reshape(rows, share)
        pieces = []
        for own, got in ((own_0, got_0), (own_1, got_1)):
            pair = (own.astype(f32) + got.astype(f32)).astype(bf16)
            both = swapped(spread_sums(pair, "head")[None], second, "head")
            pieces.append(both.reshape(-1, share))
        cut = rows // 2
        grad_projected = jnp.concatenate([pieces[1][:cut], pieces[0], pieces[1][cut:]])
        first, second_dots = (dots.reshape(-1) for dots in dots_of(unit_dot))
        unit_dot = jnp.concatenate([second_dots[:cut], first, second_dots[cut:]])
        hidden_own = lax.dynamic_slice_in_dim(hidden_in, first_col, share, 1).astype(f32)
        gain_own = lax.dynamic_slice_in_dim(norm_gain, first_col, share, 0)
        scale_col = scale_in[:, :1]
        normal_own = hidden_own * scale_col
        grad_unit = grad_projected * gain_own[None, :]
        grad_input = scale_col * (grad_unit - normal_own * (unit_dot / width)[:, None])
        out_grad_own = lax.dynamic_slice_in_dim(out_grad, first_col, share, 1)
        grad_input = grad_input + out_grad_own.astype(f32)

    head_rows = sums[:3, 384:512].reshape(3, heads, head_size)
    return (
        block_out,
        grad_input,
        grad_norm_gain,
        grad_gate_proj,
        grad_value_proj,
        grad_state_proj,
        grad_step_proj,
        sums[:4, :128],
        sums[4, :128],
        state_sums[:4],
        state_sums[4],
        head_rows[0, :, 0],
        head_rows[1, :, 0],
        jnp.sum(head_rows[2], axis=1),
        sums[5, :128],
        grad_out_proj,
    )


def solution(mesh):
    in_specs = (
        P("seq", None), P(), P(None, "head"), P(None, "head"), P(), P(None, "head"),
        P(None, "head"), P("head"), P(), P(), P("head"), P("head"), P("head"), P("head"),
        P("head", None), P("seq", None),
    )
    out_specs = (
        P("seq", "head"), P("seq", "head"), P("head"), P(None, "head"), P(None, "head"),
        P("head", None), P(None, "head"), P(None, "head"), P("head"), P(), P(), P("head"),
        P("head"), P("head"), P("head"), P("head", None),
    )
    return jax.shard_map(block, mesh=mesh, in_specs=in_specs, out_specs=out_specs, check_vma=False)
```

```python
from functools import partial

import jax
import jax.numpy as jnp
from jax import lax
from jax.experimental import pallas as pl
from jax.experimental.pallas import tpu as pltpu
from jax.experimental.layout import Layout, with_layout_constraint
from jax.sharding import PartitionSpec as P


SPAN = 256
BLOCK = 512
epsilon = 1e-05
f32 = jnp.float32
bf16 = jnp.bfloat16


def mm(a, b):
    return jnp.dot(a, b, preferred_element_type=f32)


def mm_nt(a, b):
    return lax.dot_general(a, b, (((1,), (1,)), ((), ())), preferred_element_type=f32)


def mm_tn(a, b):
    return lax.dot_general(a, b, (((0,), (0,)), ((), ())), preferred_element_type=f32)


def halves(x):
    high = x.astype(bf16)
    return jnp.concatenate([high, (x - high.astype(f32)).astype(bf16)], axis=1)


def two(x):
    high = x.astype(bf16)
    return high, (x - high.astype(f32)).astype(bf16)


def left_terms(x, axis):
    high, low = two(x)
    return jnp.concatenate([high, high, low], axis=axis)


def right_terms(x):
    high, low = two(x)
    return jnp.concatenate([high, low, high], axis=0)


def wide_terms(x):
    high, low = two(x)
    return jnp.concatenate([high, low, high], axis=1)


def folded(x):
    width = x.shape[1] // 2
    return x[:, :width] + x[:, width:]


def logistic(x):
    return 0.5 + 0.5 * jnp.tanh(0.5 * x)


def softplus(x):
    return jnp.maximum(x, 0.0) + jnp.log1p(jnp.exp(-jnp.abs(x)))


def iota(shape, axis):
    return lax.broadcasted_iota(jnp.int32, shape, axis)


def params(mebibytes):
    return pltpu.CompilerParams(
        dimension_semantics=("arbitrary",), vmem_limit_bytes=mebibytes << 20
    )


def spec(shape, index):
    return pl.BlockSpec(shape, index)


def whole_block(array):
    rank = array.ndim
    return pl.BlockSpec(array.shape, lambda *i: (0,) * rank)


def project_kernel(
    hidden_ref, gain_ref, gate_ref, value_ref, state_ref, step_ref,
    projected_ref, gate_out, stream_out, step_out, scale_out, scale_row_out, weights,
):
    @pl.when(pl.program_id(0) == 0)
    def _():
        weights[:, 0:128] = gate_ref[...]
        weights[:, 128:256] = value_ref[...]
        weights[:, 256:512] = state_ref[...]
        weights[:, 512:640] = step_ref[...]

    hidden = hidden_ref[...].astype(f32)
    scale = lax.rsqrt(jnp.mean(hidden * hidden, axis=1, keepdims=True) + epsilon)
    projected = (hidden * scale * gain_ref[...]).astype(bf16)
    projected_ref[...] = projected
    wide_scale = jnp.broadcast_to(scale, scale_out.shape)
    scale_out[...] = wide_scale
    scale_row_out[...] = wide_scale.T[0:1]
    result = mm(projected, weights[...])
    gate_out[...] = result[:, 0:128]
    stream_out[...] = result[:, 128:512].astype(bf16)
    step_out[...] = result[:, 512:640]


def project(hidden_in, norm_gain, gate_proj, value_proj, state_proj, step_wide):
    rows, width = hidden_in.shape
    span = 512
    row = lambda i: (i, 0)
    gain = norm_gain[None, :]
    return pl.pallas_call(
        project_kernel,
        grid=(rows // span,),
        in_specs=[
            spec((span, width), row), whole_block(gain), whole_block(gate_proj),
            whole_block(value_proj), whole_block(state_proj), whole_block(step_wide),
        ],
        out_specs=[
            spec((span, width), row), spec((span, 128), row), spec((span, 384), row),
            spec((span, 128), row), spec((span, 128), row), spec((1, span), lambda i: (0, i)),
        ],
        out_shape=[
            jax.ShapeDtypeStruct((rows, width), bf16),
            jax.ShapeDtypeStruct((rows, 128), f32),
            jax.ShapeDtypeStruct((rows, 384), bf16),
            jax.ShapeDtypeStruct((rows, 128), f32),
            jax.ShapeDtypeStruct((rows, 128), f32),
            jax.ShapeDtypeStruct((1, rows), f32),
        ],
        scratch_shapes=[pltpu.VMEM((width, 640), bf16)],
        compiler_params=params(56),
        cost_estimate=pl.CostEstimate(
            flops=2 * rows * width * 640, bytes_accessed=rows * width * 4, transcendentals=0
        ),
    )(hidden_in, gain, gate_proj, value_proj, state_proj, step_wide)


def convolved(ext, taps, bias):
    span = SPAN
    total = bias + taps[0:1] * ext[5 : 5 + span]
    for tap in range(1, 4):
        total = total + taps[tap : tap + 1] * ext[5 + tap : 5 + tap + span]
    return total


def running_sums(log_decay):
    span = log_decay.shape[0]
    lower = (iota((span, span), 0) >= iota((span, span), 1)).astype(bf16)
    return folded(mm(lower, halves(log_decay)))


def decay_matrix(running, running_rows, head):
    span = running.shape[0]
    at = 64 * head
    spread = running[:, at : at + 1] - running_rows[at : at + 1, :]
    return jnp.exp(jnp.where(iota((span, span), 0) >= iota((span, span), 1), spread, -jnp.inf))


def forward_kernel(
    stream_ref, edge_ref, step_ref, taps_ref, bias_ref, step_bias_ref, rate_ref, skip_ref,
    mixed_out, active_out, slope_out, reach_out, steps_out, states_out,
    ext, state, offset,
):
    span = SPAN
    first = pl.program_id(0) == 0

    @pl.when(first)
    def _():
        ext[0:8] = edge_ref[...].astype(f32)
        state[...] = jnp.zeros_like(state)
        offset[...] = jnp.zeros_like(offset)

    ext[8 : 8 + span] = stream_ref[...].astype(f32)
    conv = convolved(ext, taps_ref[...], bias_ref[...])
    ext[0:8] = ext[span : span + 8]
    chance = logistic(conv)
    active = conv * chance
    active_out[...] = active
    slope_out[...] = chance * (1.0 + conv * (1.0 - chance))
    values = active[:, 0:128]
    keys = active[:, 128:256]
    queries = active[:, 256:384]
    step = step_ref[...] + step_bias_ref[...]
    widths = softplus(step)
    running = running_sums(-rate_ref[...] * widths)
    steps_out[:, 0:128] = widths
    steps_out[:, 128:256] = running
    steps_out[:, 256:384] = logistic(step)
    running_rows = running.T
    last = running[span - 1 : span, :]
    fed = widths * values
    fed16 = fed.astype(bf16)
    query_terms = left_terms(queries, 1)
    scores = mm_nt(queries.astype(bf16), keys.astype(bf16))
    low = iota((span, 128), 1) < 64
    heads = [
        mm((scores * decay_matrix(running, running_rows, head)).astype(bf16), fed16)
        for head in range(2)
    ]
    before = state[...]
    mixed = jnp.where(low, heads[0], heads[1])
    mixed = mixed + jnp.exp(running) * mm_nt(query_terms, wide_terms(before))
    mixed_out[...] = mixed + skip_ref[...] * values
    reach_out[...] = running + offset[0:1]
    offset[...] = offset[...] + last
    tails = left_terms(jnp.exp(last - running) * fed, 0)
    after = jnp.exp(running_rows[:, span - 1 : span]) * before + mm_tn(tails, right_terms(keys))
    state[...] = after
    states_out[0] = after


def scan_forward(stream, edge, step, taps, bias, step_bias, rate, skip):
    rows = stream.shape[0]
    span = SPAN
    count = rows // span
    row = lambda i: (i, 0)
    narrow, full = spec((span, 128), row), spec((span, 384), row)
    return pl.pallas_call(
        forward_kernel,
        grid=(count,),
        in_specs=[
            full, whole_block(edge), narrow, whole_block(taps), whole_block(bias),
            whole_block(step_bias), whole_block(rate), whole_block(skip),
        ],
        out_specs=[
            narrow, full, full, narrow, full, spec((1, 128, 128), lambda i: (i, 0, 0)),
        ],
        out_shape=[
            jax.ShapeDtypeStruct((rows, 128), f32),
            jax.ShapeDtypeStruct((rows, 384), f32),
            jax.ShapeDtypeStruct((rows, 384), f32),
            jax.ShapeDtypeStruct((rows, 128), f32),
            jax.ShapeDtypeStruct((rows, 384), f32),
            jax.ShapeDtypeStruct((count, 128, 128), f32),
        ],
        scratch_shapes=[
            pltpu.VMEM((span + 8, 384), f32), pltpu.VMEM((128, 128), f32), pltpu.VMEM((8, 128), f32),
        ],
        compiler_params=params(56),
        cost_estimate=pl.CostEstimate(
            flops=count * 2 * span * span * 900, bytes_accessed=rows * 128 * 50, transcendentals=0
        ),
    )(stream, edge, step, taps, bias, step_bias, rate, skip)


def join_kernel(
    mixed_ref, query_ref, reach_ref, gate_ref, grad_ref, carried_ref, gain_ref, mixed_out, sums_out
):
    inner = mm_nt(left_terms(query_ref[...], 1), wide_terms(carried_ref[...]))
    mixed = mixed_ref[...] + jnp.exp(reach_ref[...]) * inner
    mixed_out[...] = mixed
    gate = gate_ref[...]
    gated = mixed * (gate * logistic(gate))
    at = 2 * pl.program_id(0)
    sums_out[pl.ds(at, 1), :] = jnp.sum((gated * gated).T, axis=0, keepdims=True)
    product = grad_ref[...] * gain_ref[...] * gated
    sums_out[pl.ds(at + 1, 1), :] = jnp.sum(product.T, axis=0, keepdims=True)


def join(mixed, active, reach, gate, grad, carried, gain):
    rows = mixed.shape[0]
    block = 1024
    sums = (2 * rows // block, block)
    blocks = spec((block, 128), lambda i: (i, 0))
    return pl.pallas_call(
        join_kernel,
        grid=(rows // block,),
        in_specs=[
            blocks, spec((block, 128), lambda i: (i, 2)), blocks, blocks, blocks,
            whole_block(carried), whole_block(gain),
        ],
        out_specs=[blocks, spec(sums, lambda i: (0, 0))],
        out_shape=[jax.ShapeDtypeStruct((rows, 128), f32), jax.ShapeDtypeStruct(sums, f32)],
        compiler_params=params(56),
        cost_estimate=pl.CostEstimate(
            flops=2 * rows * 128 * 128, bytes_accessed=rows * 128 * 22, transcendentals=0
        ),
    )(mixed, active, reach, gate, grad, carried, gain)


def gate_kernel(
    inner_width,
    mixed_ref, query_ref, reach_ref, gate_ref, grad_ref, sums_ref, gain_ref,
    rows_out, gate_out, mixed_grad_out, gain_out, incoming_out,
):
    @pl.when(pl.program_id(0) == 0)
    def _():
        gain_out[...] = jnp.zeros_like(gain_out)
        incoming_out[...] = jnp.zeros_like(incoming_out)

    block = mixed_ref.shape[0]
    at = 2 * pl.program_id(0)
    square = jnp.broadcast_to(sums_ref[pl.ds(at, 1), :], (128, block)).T
    product = jnp.broadcast_to(sums_ref[pl.ds(at + 1, 1), :], (128, block)).T
    scale = lax.rsqrt(square / inner_width + epsilon)
    gate = gate_ref[...]
    chance = logistic(gate)
    act = gate * chance
    mixed = mixed_ref[...]
    hat = mixed * act * scale
    rows_out[...] = (hat * gain_ref[...]).astype(bf16)
    grad = grad_ref[...]
    gain_out[...] += jnp.sum(grad * hat, axis=0, keepdims=True)
    pre = scale * (grad * gain_ref[...] - hat * (product * scale / inner_width))
    mixed_grad = pre * act
    mixed_grad_out[...] = mixed_grad
    gate_out[...] = (pre * mixed * (chance * (1.0 + gate * (1.0 - chance)))).astype(bf16)
    incoming_out[...] += mm_tn(
        left_terms(jnp.exp(reach_ref[...]) * mixed_grad, 0), right_terms(query_ref[...])
    )


def gate_step(mixed, active, reach, gate, grad, sums, gain, inner_width):
    rows = mixed.shape[0]
    block = sums.shape[1]
    blocks = spec((block, 128), lambda i: (i, 0))
    return pl.pallas_call(
        partial(gate_kernel, inner_width),
        grid=(rows // block,),
        in_specs=[
            blocks, spec((block, 128), lambda i: (i, 2)), blocks, blocks, blocks, whole_block(sums),
            whole_block(gain),
        ],
        out_specs=[
            blocks, blocks, blocks, spec((1, 128), lambda i: (0, 0)),
            spec((128, 128), lambda i: (0, 0)),
        ],
        out_shape=[
            jax.ShapeDtypeStruct((rows, 128), bf16),
            jax.ShapeDtypeStruct((rows, 128), bf16),
            jax.ShapeDtypeStruct((rows, 128), f32),
            jax.ShapeDtypeStruct((1, 128), f32),
            jax.ShapeDtypeStruct((128, 128), f32),
        ],
        compiler_params=params(56),
        cost_estimate=pl.CostEstimate(
            flops=2 * rows * 128 * 128, bytes_accessed=rows * 128 * 26, transcendentals=0
        ),
    )(mixed, active, reach, gate, grad, sums, gain)


def head_sums(x):
    same = (iota((128, 128), 0) < 64) == (iota((128, 128), 1) < 64)
    ones = same.astype(bf16)
    high = x.astype(bf16)
    return mm(high, ones) + mm((x - high.astype(f32)).astype(bf16), ones)


def backward_kernel(
    first_chunk,
    stream_ref, before_ref, edge_ref, active_ref, slope_ref, steps_ref, taps_ref, rate_ref, skip_ref,
    mixed_ref, grad_ref, reach_ref, start_ref, end_ref, carried_ref, arriving_ref, next_ref,
    stream_grad_out, tail_out, head_out, sums_out, leaving_out,
    ext, grads, state_grad,
):
    span = SPAN
    chunk = first_chunk - pl.program_id(0)

    @pl.when(pl.program_id(0) == 0)
    def _():
        state_grad[...] = arriving_ref[...]
        grads[span : span + 8] = next_ref[...]
        sums_out[...] = jnp.zeros_like(sums_out)

    @pl.when(chunk == 0)
    def _():
        ext[0:8] = edge_ref[...].astype(f32)

    @pl.when(chunk > 0)
    def _():
        ext[0:8] = before_ref[8:16].astype(f32)

    ext[8 : 8 + span] = stream_ref[...].astype(f32)
    taps = taps_ref[...]
    values = active_ref[:, 0:128]
    keys = active_ref[:, 128:256]
    queries = active_ref[:, 256:384]
    keys16 = keys.astype(bf16)
    rate = rate_ref[...]
    widths = steps_ref[:, 0:128]
    running = steps_ref[:, 128:256]
    running_rows = running.T
    last = running[span - 1 : span, :]
    fed = widths * values
    fed16 = fed.astype(bf16)
    grad = grad_ref[...]
    grad16 = grad.astype(bf16)
    scores = mm_nt(queries.astype(bf16), keys16)
    low = iota((span, 128), 1) < 64
    grad_turned = pltpu.roll(grad, 64, 1)
    fed_turned = pltpu.roll(fed, 64, 1)
    score_grad = None
    fed_grads = []
    for head in range(2):
        decay = decay_matrix(running, running_rows, head)
        mine = low == (head == 0)
        grad_high, grad_low = two(jnp.where(mine, grad, grad_turned))
        left = [jnp.where(low, grad_high, grad_low), jnp.where(low, grad_high, 0)]
        right = two(jnp.where(mine, fed, fed_turned))
        part = mm_nt(jnp.concatenate(left, axis=1), jnp.concatenate(right, axis=1)) * decay
        score_grad = part if score_grad is None else score_grad + part
        fed_grads.append(mm_tn((scores * decay).astype(bf16), grad16))

    offset = (reach_ref[span - 8 : span, :] - running[span - 8 : span, :]).T[:, 7:8]
    carried = jnp.exp(offset) * carried_ref[...]
    before = jnp.where(chunk > 0, start_ref[0], 0.0) + carried
    last_rows = jnp.exp(running_rows[:, span - 1 : span])
    after = end_ref[0] + last_rows * carried
    after_grad = state_grad[...]
    tail = jnp.exp(last - running)
    reached = jnp.exp(running) * grad
    query_terms = right_terms(queries)
    fed_grad = jnp.where(low, fed_grads[0], fed_grads[1])
    fed_grad = fed_grad + tail * mm_nt(keys16, after_grad.astype(bf16))
    score_high, score_low = two(score_grad)
    query_grad = mm(
        jnp.concatenate([score_high, score_high, score_low], axis=1), right_terms(keys)
    ) + mm(left_terms(reached, 1), right_terms(before))
    key_grad = mm_tn(
        jnp.concatenate([score_high, score_high, score_low], axis=0), query_terms
    ) + mm(left_terms(tail * fed, 1), right_terms(after_grad))
    leaving = last_rows * after_grad + mm_tn(left_terms(reached, 0), query_terms)
    state_grad[...] = leaving
    leaving_out[...] = leaving
    value_grad = widths * fed_grad + skip_ref[...] * grad

    mixed = mixed_ref[...] - skip_ref[...] * values
    balance = head_sums(grad16.astype(f32) * mixed - fed16.astype(f32) * fed_grad)
    upper = (iota((span, span), 0) <= iota((span, span), 1)).astype(bf16)
    boundary = head_sums(
        jnp.broadcast_to(jnp.sum((after_grad * after).T, axis=0, keepdims=True), (8, 128))
    )
    decay_grad = folded(mm(upper, halves(balance))) + boundary[0:1]
    width_grad = head_sums(values * fed_grad) - rate * decay_grad
    step_grad = width_grad * steps_ref[:, 256:384]
    sums_out[0:1, 384:512] += jnp.sum(step_grad, axis=0, keepdims=True)
    sums_out[1:2, 384:512] += jnp.sum(-widths * decay_grad, axis=0, keepdims=True)
    sums_out[2:3, 384:512] += jnp.sum(grad * values, axis=0, keepdims=True)

    conv_grad = jnp.concatenate([value_grad, key_grad, query_grad], axis=1) * slope_ref[...]
    grads[0:span] = conv_grad
    for tap in range(4):
        sums_out[tap : tap + 1, 0:384] += jnp.sum(
            conv_grad * ext[5 + tap : 5 + tap + span], axis=0, keepdims=True
        )
    sums_out[4:5, 0:384] += jnp.sum(conv_grad, axis=0, keepdims=True)
    stream_grad = taps[3:4] * conv_grad
    for tap in range(3):
        stream_grad = stream_grad + taps[tap : tap + 1] * grads[3 - tap : 3 - tap + span]
    high = stream_grad.astype(bf16)
    stream_grad_out[:, 0:384] = high
    stream_grad_out[:, 384:512] = step_grad.astype(bf16)
    stream_grad_out[:, 512:768] = (stream_grad - high.astype(f32))[:, 128:384].astype(bf16)

    @pl.when(pl.program_id(0) == 0)
    def _():
        tail_out[...] = stream_grad[span - 8 :]

    head_out[...] = conv_grad[0:8]
    grads[span : span + 8] = conv_grad[0:8]


def scan_backward(
    late, stream, edge, active, slope, steps, taps, rate, skip, mixed, grad, reach, states, carried,
    arriving, next_rows,
):
    rows = stream.shape[0]
    span = SPAN
    count = rows // span // 2
    first = 2 * count - 1 if late else count - 1
    row = lambda i: (first - i, 0)
    fixed = lambda i: (0, 0)
    narrow, full = spec((span, 128), row), spec((span, 384), row)
    return pl.pallas_call(
        partial(backward_kernel, first),
        grid=(count,),
        in_specs=[
            full, spec((16, 384), lambda i: (jnp.maximum((first - i) * (span // 16) - 1, 0), 0)),
            whole_block(edge), full, full, full, whole_block(taps), whole_block(rate),
            whole_block(skip), narrow, narrow, narrow,
            spec((1, 128, 128), lambda i: (jnp.maximum(first - 1 - i, 0), 0, 0)),
            spec((1, 128, 128), lambda i: (first - i, 0, 0)),
            whole_block(carried), whole_block(arriving), whole_block(next_rows),
        ],
        out_specs=[
            spec((span, 768), lambda i: (count - 1 - i, 0)), spec((8, 384), fixed),
            spec((8, 384), fixed), spec((8, 512), fixed), spec((128, 128), fixed),
        ],
        out_shape=[
            jax.ShapeDtypeStruct((rows // 2, 768), bf16),
            jax.ShapeDtypeStruct((8, 384), f32),
            jax.ShapeDtypeStruct((8, 384), f32),
            jax.ShapeDtypeStruct((8, 512), f32),
            jax.ShapeDtypeStruct((128, 128), f32),
        ],
        scratch_shapes=[
            pltpu.VMEM((span + 8, 384), f32), pltpu.VMEM((span + 8, 384), f32),
            pltpu.VMEM((128, 128), f32),
        ],
        compiler_params=params(56),
        cost_estimate=pl.CostEstimate(
            flops=count * 2 * span * span * 1500, bytes_accessed=rows * 128 * 30, transcendentals=0
        ),
    )(
        stream, stream, edge, active, slope, steps, taps, rate, skip, mixed, grad, reach, states,
        states, carried, arriving, next_rows,
    )


def group_of(rows, index):
    half = rows // BLOCK // 2
    if index == 0:
        return half - 1, lambda place: half + place
    return half + 1, lambda place: jnp.where(place < half, place, place + half - 1)


def parts_kernel(
    block_of, last_block, early_blocks,
    place_ref, gate_ref, early_ref, late_ref, weights_ref, hidden_ref, scale_ref, gain_ref, tail_ref,
    next_ref, taps_ref,
    own_out, other_out, dots_out, sums_out,
    left, edge,
):
    at_block = block_of(pl.program_id(0))

    @pl.when(pl.program_id(0) == 0)
    def _():
        sums_out[...] = jnp.zeros_like(sums_out)

    block = left.shape[0]
    left[:, 0:128] = gate_ref[...]

    @pl.when(at_block < early_blocks)
    def _():
        left[:, 128:640] = early_ref[...]

    @pl.when(at_block >= early_blocks)
    def _():
        left[:, 128:640] = late_ref[...]

    @pl.when(at_block == last_block)
    def _():
        edge[0:8] = jnp.zeros_like(edge[0:8])
        edge[8:16] = next_ref[...]
        fixed = tail_ref[...]
        for tap in range(3):
            fixed = fixed + taps_ref[tap : tap + 1] * edge[3 - tap : 11 - tap]
        left[block - 8 :, 128:512] = fixed.astype(bf16)

    chips, share, _ = own_out.shape
    total = mm(left[...], weights_ref[...]).astype(bf16)
    scale = scale_ref[...]
    summed = None
    turned = []
    for at in range(0, total.shape[1], 128):
        lanes = slice(at, at + 128)
        part = total[:, lanes].astype(f32)
        turned.append(part.T)
        product = part * (hidden_ref[:, lanes].astype(f32) * scale)
        sums_out[0:1, lanes] += jnp.sum(product, axis=0, keepdims=True)
        product = product * gain_ref[:, lanes]
        summed = product if summed is None else summed + product
    dots_out[...] = jnp.sum(summed.T, axis=0, keepdims=True)
    turned = jnp.concatenate(turned, axis=0)
    second = place_ref[1] == 1
    for chip in range(chips):
        low = turned[2 * chip * share : (2 * chip + 1) * share]
        high = turned[(2 * chip + 1) * share : (2 * chip + 2) * share]
        own_out[chip] = jnp.where(second, high, low).astype(bf16)
        other_out[chip] = jnp.where(second, low, high).astype(bf16)


def input_parts(
    index, place, gate16, early16, late16, weights, hidden_in, scale, gain, tail, next_head, taps,
    chips,
):
    rows, width = hidden_in.shape
    block = BLOCK
    count, block_of = group_of(rows, index)
    blocks = rows // block
    row = lambda i, at: (block_of(i), 0)
    share = width // chips // 2
    turned = spec((chips, share, block), lambda i, at: (0, 0, i))
    return pl.pallas_call(
        partial(parts_kernel, block_of, blocks - 1, blocks // 2),
        grid_spec=pltpu.PrefetchScalarGridSpec(
            num_scalar_prefetch=1,
            grid=(count,),
            in_specs=[
                spec((block, 128), row),
                spec((block, 512), lambda i, at: (jnp.minimum(block_of(i), blocks // 2 - 1), 0)),
                spec((block, 512), lambda i, at: (jnp.maximum(block_of(i) - blocks // 2, 0), 0)),
                whole_block(weights), spec((block, width), row), spec((block, 128), row),
                whole_block(gain), whole_block(tail), whole_block(next_head), whole_block(taps),
            ],
            out_specs=[
                turned, turned, spec((1, block), lambda i, at: (0, i)),
                spec((1, width), lambda i, at: (0, 0)),
            ],
            scratch_shapes=[pltpu.VMEM((block, 640), bf16), pltpu.VMEM((16, 384), f32)],
        ),
        out_shape=[
            jax.ShapeDtypeStruct((chips, share, count * block), bf16),
            jax.ShapeDtypeStruct((chips, share, count * block), bf16),
            jax.ShapeDtypeStruct((1, count * block), f32),
            jax.ShapeDtypeStruct((1, width), f32),
        ],
        compiler_params=params(56),
        cost_estimate=pl.CostEstimate(
            flops=2 * count * block * width * 640, bytes_accessed=count * block * width * 5,
            transcendentals=0,
        ),
    )(
        place, gate16, early16, late16, weights, hidden_in, scale, gain, tail, next_head, taps
    )


def output_kernel(at_ref, rows_ref, weights_ref, hidden_ref, parts_out):
    groups, share, _ = parts_out.shape
    summed = None
    for group in range(rows_ref.shape[0]):
        term = mm(rows_ref[group], weights_ref[group]).astype(bf16).astype(f32)
        summed = term if summed is None else summed + term
    total = hidden_ref[...].astype(f32) + summed
    turned = [total[:, at : at + 128].T for at in range(0, total.shape[1], 128)]
    turned = jnp.concatenate(turned, axis=0)
    for group in range(groups):
        parts_out[group] = turned[group * share : (group + 1) * share].astype(bf16)


def output_rows(rows, weights, hidden, at):
    groups, tokens, inner = rows.shape
    width = hidden.shape[1]
    block = min(tokens, SPAN)
    steps = tokens // block
    share = width // groups
    return pl.pallas_call(
        output_kernel,
        grid_spec=pltpu.PrefetchScalarGridSpec(
            num_scalar_prefetch=1,
            grid=(steps,),
            in_specs=[
                spec((groups, block, inner), lambda i, at: (0, i, 0)), whole_block(weights),
                spec((block, width), lambda i, at: (steps * at[0] + i, 0)),
            ],
            out_specs=spec((groups, share, block), lambda i, at: (0, 0, i)),
        ),
        out_shape=jax.ShapeDtypeStruct((groups, share, tokens), bf16),
        compiler_params=params(56),
        cost_estimate=pl.CostEstimate(
            flops=2 * tokens * groups * inner * width, bytes_accessed=8 << 20, transcendentals=0
        ),
    )(at, rows, weights, hidden)


def side_kernel(blocks_ref, out_ref):
    tokens = blocks_ref.shape[2]
    for at in range(blocks_ref.shape[0]):
        out_ref[:, at * tokens : (at + 1) * tokens] = blocks_ref[at]


def side_by_side(blocks):
    count, share, tokens = blocks.shape
    return pl.pallas_call(
        side_kernel,
        grid=(count // 2,),
        in_specs=[spec((2, share, tokens), lambda i: (i, 0, 0))],
        out_specs=spec((share, 2 * tokens), lambda i: (0, i)),
        out_shape=jax.ShapeDtypeStruct((share, count * tokens), blocks.dtype),
        compiler_params=params(56),
    )(blocks)


def row_major(x):
    return with_layout_constraint(x, Layout(major_to_minor=(0, 1)))


def passed_along(block, axis, distance):
    devices = range(lax.axis_size(axis))
    route = [(i - distance, i) for i in devices if i - distance in devices]
    return lax.ppermute(block, axis, route)


def bits_of(axis):
    count = lax.axis_size(axis)
    assert count & (count - 1) == 0
    return [1 << n for n in range(count.bit_length() - 1)]


def summed_over(value, axis, turned=False):
    count = lax.axis_size(axis)
    bits = bits_of(axis)
    for bit in reversed(bits) if turned else bits:
        value = value + lax.ppermute(value, axis, [(i, i ^ bit) for i in range(count)])
    return value


def spread_sums(pair, axis):
    chips = pair.shape[0]
    mine = lax.axis_index(axis)
    spread = jnp.stack([pair, jnp.zeros_like(pair)], axis=1)
    spread = jnp.where(mine % 2 == 0, spread, spread[:, ::-1])
    spread = spread.reshape(2 * chips, *pair.shape[1:])
    return lax.psum_scatter(spread, axis, scatter_dimension=0, tiled=False).astype(f32)


def line_kernel(at_ref, up_own, up_got, down_own, down_got, *refs):
    up_out, down_out = refs[-2:]
    up = up_own[0].astype(f32) + up_got[0].astype(f32)
    down = down_own[0].astype(f32) + down_got[0].astype(f32)
    if len(refs) == 4:
        up, down = up + refs[0][...].astype(f32), down + refs[1][...].astype(f32)
    up_out[...] = up.astype(bf16)
    down_out[...] = down.astype(bf16)


def line_step(up_at, down_at, own, got, arrived):
    chips, share, tokens = own.shape
    block = tokens // 2
    at = jnp.stack([up_at, down_at]).astype(jnp.int32)
    at = jnp.clip(at, 0, chips - 1)
    blocks = [spec((1, share, block), lambda i, at, k=k: (at[k], 0, i)) for k in (0, 0, 1, 1)]
    plain = spec((share, block), lambda i, at: (0, i))
    return pl.pallas_call(
        line_kernel,
        grid_spec=pltpu.PrefetchScalarGridSpec(
            num_scalar_prefetch=1,
            grid=(2,),
            in_specs=blocks + [plain] * len(arrived),
            out_specs=[plain, plain],
        ),
        out_shape=[jax.ShapeDtypeStruct((share, tokens), bf16)] * 2,
        compiler_params=params(56),
        cost_estimate=pl.CostEstimate(
            flops=share * tokens * 4, bytes_accessed=share * tokens * 16, transcendentals=0
        ),
    )(at, own, got, own, got, *arrived)


def line_sent(step, sent, axis):
    chips, cores = 4, 2
    last = chips * cores - 1
    up = lax.ppermute(sent[0], axis, [(i, i + cores) for i in range(cores * step)])
    down_route = [(last - i, last - i - cores) for i in range(cores * step)]
    down = lax.ppermute(sent[1], axis, down_route)
    return up, down


def line_terms(step, own, got, arrived, axis):
    chip = lax.axis_index(axis) // 2
    return line_step(4 + chip - step, step - 4 + chip, own, got, arrived)


after = lax.optimization_barrier


def own_features(rows, second):
    share = rows.shape[1] // 2
    turned = [rows[:, at : at + 128].T for at in range(0, 2 * share, 128)]
    turned = jnp.concatenate(turned, axis=0)
    return jnp.where(second, turned[share:], turned[:share])


def finish_kernel(
    width,
    place_ref, own_ref, got_ref, up_ref, down_ref, hidden_ref, scale_ref, gain_ref, dots_ref,
    grad_ref, *refs,
):
    out_ref = refs[-1]
    second = place_ref[1] == 1
    total = own_ref[0].astype(f32) + got_ref[0].astype(f32)
    total = total + up_ref[...].astype(f32) + down_ref[...].astype(f32)
    gain = jnp.broadcast_to(gain_ref[...], (8, gain_ref.shape[1]))
    gain = own_features(gain, second)[:, 0:1]
    scale = scale_ref[...]
    dot = dots_ref[...] * (1.0 / width) * (scale * scale)
    normal = own_features(hidden_ref[...].astype(f32), second)
    base = own_features(grad_ref[...].astype(f32), second) - normal * dot
    out_ref[...] = base + total * (gain * scale)


def finish(index, own, got, up, down, hidden_in, scale, gain, dots, out_grad, place, target):
    rows, width = hidden_in.shape
    share = own.shape[1]
    both = 2 * share
    block = BLOCK
    count, block_of = group_of(rows, index)
    here = spec((1, share, block), lambda i, at: (at[0], 0, i))
    plain = spec((share, block), lambda i, at: (0, i))
    feature = spec((block, both), lambda i, at: (block_of(i), at[0]))
    operands = [place, own, got, up, down, hidden_in, scale, gain, dots, out_grad]
    in_specs = [
        here, here, plain, plain, feature, spec((1, block), lambda i, at: (0, block_of(i))),
        spec((1, both), lambda i, at: (0, at[0])), spec((1, block), lambda i, at: (0, i)), feature,
    ]
    aliases = {}
    if target is not None:
        aliases = {len(operands): 0}
        operands.append(target)
        in_specs.append(pl.BlockSpec(memory_space=pl.ANY))
    return pl.pallas_call(
        partial(finish_kernel, width),
        grid_spec=pltpu.PrefetchScalarGridSpec(
            num_scalar_prefetch=1,
            grid=(count,),
            in_specs=in_specs,
            out_specs=spec((share, block), lambda i, at: (0, block_of(i))),
        ),
        out_shape=jax.ShapeDtypeStruct((share, rows), f32),
        input_output_aliases=aliases,
        compiler_params=params(56),
        cost_estimate=pl.CostEstimate(
            flops=rows * both * 5, bytes_accessed=count * block * both * 12, transcendentals=0
        ),
    )(*operands)


def chained(states, decays, mine, backward):
    count = states.shape[0]
    order = range(count)
    if backward:
        order = reversed(order)
    total = jnp.zeros_like(states[0])
    for at in order:
        use = at > mine if backward else at < mine
        total = jnp.where(use, decays[at][:, None] * total + states[at], total)
    return total


def block(
    hidden_in, norm_gain, gate_proj, value_proj, state_proj, step_proj, conv_value,
    conv_value_bias, conv_state, conv_state_bias, step_bias, decay_rate, skip_gain, mix_gain,
    out_proj, out_grad,
):
    rows, width = hidden_in.shape
    groups = lax.axis_size("head")
    share = width // groups
    mine = lax.axis_index("head")
    first_col = mine * share
    chips = groups // 2
    core = mine % 2
    inner_local = gate_proj.shape[1]
    inner_width = inner_local * groups
    heads = step_proj.shape[1]
    head_size = inner_local // heads

    def wide(x):
        return jnp.repeat(x, head_size, axis=-1)

    step_wide = wide(step_proj)
    rate, skip, step_shift = (wide(x)[None, :] for x in (decay_rate, skip_gain, step_bias))
    taps = jnp.concatenate([conv_value, conv_state], axis=1)
    bias = jnp.concatenate([conv_value_bias, conv_state_bias])[None, :]
    gain = mix_gain[None, :]

    all_out_proj = lax.all_gather(out_proj, "head")
    projected, gate_in, stream, step, scale_in, scale_row = project(
        hidden_in, norm_gain, gate_proj, value_proj, state_proj, step_wide
    )
    edge = passed_along(stream[rows - 8 :], "seq", 1)
    grad_gated = lax.dot_general(
        out_grad, out_proj, (((1,), (1,)), ((), ())), preferred_element_type=f32
    )
    partial_mixed, active, slope, reach, steps, states = scan_forward(
        stream, edge, step, taps, bias, step_shift, rate, skip
    )
    at_seq = lax.axis_index("seq")
    decay_here = jnp.exp(reach[rows - 1])
    packed = jnp.concatenate([states[-1], jnp.broadcast_to(decay_here[None, :], (8, 128))])
    gathered = lax.all_gather(packed, "seq")
    decays = gathered[:, 128]
    carried = chained(gathered[:, :128], decays, at_seq, False)
    mixed, sums = join(partial_mixed, active, reach, gate_in, grad_gated, carried, gain)
    sums = summed_over(sums, "head")
    gated_rows, grad_gate16, grad_mixed, grad_mix_gain, incoming = gate_step(
        mixed, active, reach, gate_in, grad_gated, sums, gain, inner_width
    )

    own_tokens = rows // groups
    group_rows = lax.all_to_all(
        gated_rows.reshape(groups, own_tokens, inner_local), "head", 0, 0, tiled=False
    )
    on_line = chips == 4 and 2 * share % 128 == 0
    partner = [(i, i ^ 1) for i in range(groups)]
    place = jnp.stack([mine // 2, core]).astype(jnp.int32)
    arriving = chained(lax.all_gather(incoming, "seq"), decays, at_seq, True)
    scan_args = (
        stream, edge, active, slope, steps, taps, rate, skip, mixed, grad_mixed, reach, states, carried
    )
    late16, tail, head, late_sums, arriving = scan_backward(
        True, *scan_args, arriving, jnp.zeros((8, stream.shape[1]), f32)
    )
    step_back = wide(step_proj).T * (1.0 / head_size)
    weights = jnp.concatenate(
        [gate_proj.T, value_proj.T, state_proj.T, step_back.astype(bf16)], axis=0
    )
    gain_in = norm_gain[None, :]

    def parts_of(index, early16, next_head):
        return input_parts(
            index, place, grad_gate16, early16, late16, weights, hidden_in, scale_in, gain_in, tail,
            next_head, taps, chips,
        )

    own_0, other_0, dots_0, norm_sums = parts_of(0, late16, head)
    got_0 = lax.ppermute(other_0, "head", partner)
    out_parts = output_rows(group_rows, all_out_proj, hidden_in, mine.astype(jnp.int32)[None])
    if on_line:
        line_0 = line_terms(1, own_0, got_0, (), "head")
        line_0 = line_sent(1, line_0, "head")
    out_parts = lax.all_to_all(out_parts, "head", 0, 0, tiled=False)
    early16, _, head, early_sums, _ = scan_backward(False, *scan_args, arriving, head)
    next_head = passed_along(head, "seq", -1)
    contract = (((0,), (0,)), ((), ()))

    def product(left, right):
        return lax.dot_general(left, right, contract, preferred_element_type=f32)

    gated_rows, _ = after((gated_rows, early16))
    grad_out_proj = product(gated_rows, out_grad)
    own_1, other_1, dots_1, more_sums = parts_of(1, early16, next_head)
    norm_sums = norm_sums + more_sums
    got_1 = lax.ppermute(other_1, "head", partner)
    dots = jnp.concatenate([dots_0.reshape(-1, 128), dots_1.reshape(-1, 128)], axis=0)
    needs = (late16, next_head, projected)
    if on_line:
        line_0, dots = after((line_0, dots))
        line_0 = line_terms(2, own_0, got_0, line_0, "head")
        line_0 = line_sent(2, line_0, "head")
        sent = line_terms(1, own_1, got_1, (), "head")
        sent, needs, dots = after((sent, needs, dots))
        line_1 = line_sent(1, sent, "head")
        line_0 = line_terms(3, own_0, got_0, line_0, "head")
        line_0 = line_sent(3, line_0, "head")
    sums = (late_sums + early_sums).at[5, :128].set(grad_mix_gain[0])
    headed = jnp.concatenate(
        [sums[:5, 128:384].reshape(-1, 128), norm_sums.reshape(-1, 128), dots], axis=0
    )
    headed = summed_over(headed, "head", False)
    unit_dot, headed = headed[-dots.shape[0] :], headed[: -dots.shape[0]]

    late_fixed, next_rows, projected = needs
    extra = [sum(taps[tap] * next_rows[row - tap] for tap in range(row + 1)) for row in range(3)]
    fixed = tail.at[5:].add(jnp.stack(extra))
    fixed16 = fixed.astype(bf16)
    low16 = (fixed - fixed16.astype(f32))[:, inner_local:].astype(bf16)
    late_fixed = lax.dynamic_update_slice(late_fixed, fixed16, (rows // 2 - 8, 0))
    late_fixed = lax.dynamic_update_slice(late_fixed, low16, (rows // 2 - 8, 512))
    rest16 = jnp.concatenate([early16, late_fixed], axis=0)
    grad_rest = product(projected, rest16)
    state_part = row_major(grad_rest[:, 128:384] + grad_rest[:, 512:768])
    grad_value_proj = row_major(grad_rest[:, :128])
    step_sums = row_major(grad_rest[:, 384:512]).T[::head_size]
    if on_line:
        line_1, state_part = after((line_1, state_part))
        sent = line_terms(2, own_1, got_1, line_1, "head")
        sent, projected, sums = after((sent, projected, sums))
        line_1 = line_sent(2, sent, "head")
    grad_gate_proj = row_major(product(projected, grad_gate16))
    grad_state_proj = lax.psum_scatter(state_part, "head", scatter_dimension=0, tiled=True)
    grad_state_proj = summed_over(grad_state_proj, "seq", False)
    grad_value_proj = summed_over(grad_value_proj, "seq", False)
    grad_gate_proj = summed_over(grad_gate_proj, "seq", True)
    grad_out_proj = summed_over(grad_out_proj, "seq", False)

    small = jnp.concatenate(
        [sums.reshape(-1, 128), step_sums.reshape(-1, 128), headed.reshape(-1, 128)], axis=0
    )
    small = summed_over(small, "seq", False).reshape(-1)
    at = sums.size
    sums, small = small[:at].reshape(8, 512), small[at:]
    grad_step_proj, small = small[: heads * width].reshape(heads, width).T, small[heads * width :]
    state_sums, norm_sums = small[: 5 * 256].reshape(5, 256), small[5 * 256 :]
    grad_norm_gain = lax.dynamic_slice_in_dim(norm_sums, first_col, share, 0)
    unit_dot = unit_dot.reshape(1, -1)
    dots_0, dots_1 = unit_dot[:, : dots_0.size], unit_dot[:, dots_0.size :]

    if on_line:
        sent = line_terms(3, own_1, got_1, line_1, "head")
        sent, own_0, out_parts = after((sent, own_0, out_parts))
        line_1 = line_sent(3, sent, "head")
    block_out = side_by_side(out_parts).T
    if on_line:
        grad_input = None
        for index, own, got, (up, down), dots in (
            (0, own_0, got_0, line_0, dots_0), (1, own_1, got_1, line_1, dots_1)
        ):
            grad_input = finish(
                index, own, got, up, down, hidden_in, scale_row, gain_in, dots, out_grad, place,
                grad_input,
            )
        grad_input = grad_input.T
    else:
        pieces = []
        for own, got in ((own_0, got_0), (own_1, got_1)):
            pair = (own.astype(f32) + got.astype(f32)).astype(bf16)
            pieces.append(spread_sums(pair, "head").T)
        cut = rows // 2
        grad_projected = jnp.concatenate([pieces[1][:cut], pieces[0], pieces[1][cut:]])
        dots_0, dots_1 = dots_0.reshape(-1), dots_1.reshape(-1)
        unit_dot = jnp.concatenate([dots_1[:cut], dots_0, dots_1[cut:]])
        hidden_own = lax.dynamic_slice_in_dim(hidden_in, first_col, share, 1).astype(f32)
        gain_own = lax.dynamic_slice_in_dim(norm_gain, first_col, share, 0)
        scale_col = scale_in[:, :1]
        normal_own = hidden_own * scale_col
        grad_unit = grad_projected * gain_own[None, :]
        grad_input = scale_col * (grad_unit - normal_own * (unit_dot / width)[:, None])
        out_grad_own = lax.dynamic_slice_in_dim(out_grad, first_col, share, 1)
        grad_input = grad_input + out_grad_own.astype(f32)

    head_rows = sums[:3, 384:512].reshape(3, heads, head_size)
    return (
        block_out,
        grad_input,
        grad_norm_gain,
        grad_gate_proj,
        grad_value_proj,
        grad_state_proj,
        grad_step_proj,
        sums[:4, :128],
        sums[4, :128],
        state_sums[:4],
        state_sums[4],
        head_rows[0, :, 0],
        head_rows[1, :, 0],
        jnp.sum(head_rows[2], axis=1),
        sums[5, :128],
        grad_out_proj,
    )


def solution(mesh):
    in_specs = (
        P("seq", None), P(), P(None, "head"), P(None, "head"), P(), P(None, "head"),
        P(None, "head"), P("head"), P(), P(), P("head"), P("head"), P("head"), P("head"),
        P("head", None), P("seq", None),
    )
    out_specs = (
        P("seq", "head"), P("seq", "head"), P("head"), P(None, "head"), P(None, "head"),
        P("head", None), P(None, "head"), P(None, "head"), P("head"), P(), P(), P("head"),
        P("head"), P("head"), P("head"), P("head", None),
    )
    return jax.shard_map(block, mesh=mesh, in_specs=in_specs, out_specs=out_specs, check_vma=False)
```

```python
from functools import partial

import jax
import jax.numpy as jnp
from jax import lax
from jax.experimental import pallas as pl
from jax.experimental.pallas import tpu as pltpu
from jax.experimental.layout import Layout, with_layout_constraint
from jax.sharding import PartitionSpec as P


SPAN = 256
BLOCK = 512
epsilon = 1e-05
f32 = jnp.float32
bf16 = jnp.bfloat16


def mm(a, b):
    return jnp.dot(a, b, preferred_element_type=f32)


def mm_nt(a, b):
    return lax.dot_general(a, b, (((1,), (1,)), ((), ())), preferred_element_type=f32)


def mm_tn(a, b):
    return lax.dot_general(a, b, (((0,), (0,)), ((), ())), preferred_element_type=f32)


def halves(x):
    high = x.astype(bf16)
    return jnp.concatenate([high, (x - high.astype(f32)).astype(bf16)], axis=1)


def two(x):
    high = x.astype(bf16)
    return high, (x - high.astype(f32)).astype(bf16)


def left_terms(x, axis):
    high, low = two(x)
    return jnp.concatenate([high, high, low], axis=axis)


def right_terms(x):
    high, low = two(x)
    return jnp.concatenate([high, low, high], axis=0)


def wide_terms(x):
    high, low = two(x)
    return jnp.concatenate([high, low, high], axis=1)


def folded(x):
    width = x.shape[1] // 2
    return x[:, :width] + x[:, width:]


def logistic(x):
    return 0.5 + 0.5 * jnp.tanh(0.5 * x)


def softplus(x):
    return jnp.maximum(x, 0.0) + jnp.log1p(jnp.exp(-jnp.abs(x)))


def iota(shape, axis):
    return lax.broadcasted_iota(jnp.int32, shape, axis)


def params(mebibytes):
    return pltpu.CompilerParams(
        dimension_semantics=("arbitrary",), vmem_limit_bytes=mebibytes << 20
    )


def spec(shape, index):
    return pl.BlockSpec(shape, index)


def whole_block(array):
    rank = array.ndim
    return pl.BlockSpec(array.shape, lambda *i: (0,) * rank)


def project_kernel(
    hidden_ref, gain_ref, gate_ref, value_ref, state_ref, step_ref,
    projected_ref, gate_out, stream_out, step_out, scale_out, scale_row_out, weights,
):
    @pl.when(pl.program_id(0) == 0)
    def _():
        weights[:, 0:128] = gate_ref[...]
        weights[:, 128:256] = value_ref[...]
        weights[:, 256:512] = state_ref[...]
        weights[:, 512:640] = step_ref[...]

    hidden = hidden_ref[...].astype(f32)
    scale = lax.rsqrt(jnp.mean(hidden * hidden, axis=1, keepdims=True) + epsilon)
    projected = (hidden * scale * gain_ref[...]).astype(bf16)
    projected_ref[...] = projected
    wide_scale = jnp.broadcast_to(scale, scale_out.shape)
    scale_out[...] = wide_scale
    scale_row_out[...] = wide_scale.T[0:1]
    result = mm(projected, weights[...])
    gate_out[...] = result[:, 0:128]
    stream_out[...] = result[:, 128:512].astype(bf16)
    step_out[...] = result[:, 512:640]


def project(hidden_in, norm_gain, gate_proj, value_proj, state_proj, step_wide):
    rows, width = hidden_in.shape
    span = 512
    row = lambda i: (i, 0)
    gain = norm_gain[None, :]
    return pl.pallas_call(
        project_kernel,
        grid=(rows // span,),
        in_specs=[
            spec((span, width), row), whole_block(gain), whole_block(gate_proj),
            whole_block(value_proj), whole_block(state_proj), whole_block(step_wide),
        ],
        out_specs=[
            spec((span, width), row), spec((span, 128), row), spec((span, 384), row),
            spec((span, 128), row), spec((span, 128), row), spec((1, span), lambda i: (0, i)),
        ],
        out_shape=[
            jax.ShapeDtypeStruct((rows, width), bf16),
            jax.ShapeDtypeStruct((rows, 128), f32),
            jax.ShapeDtypeStruct((rows, 384), bf16),
            jax.ShapeDtypeStruct((rows, 128), f32),
            jax.ShapeDtypeStruct((rows, 128), f32),
            jax.ShapeDtypeStruct((1, rows), f32),
        ],
        scratch_shapes=[pltpu.VMEM((width, 640), bf16)],
        compiler_params=params(56),
        cost_estimate=pl.CostEstimate(
            flops=2 * rows * width * 640, bytes_accessed=rows * width * 4, transcendentals=0
        ),
    )(hidden_in, gain, gate_proj, value_proj, state_proj, step_wide)


def convolved(ext, taps, bias):
    span = SPAN
    total = bias + taps[0:1] * ext[5 : 5 + span]
    for tap in range(1, 4):
        total = total + taps[tap : tap + 1] * ext[5 + tap : 5 + tap + span]
    return total


def running_sums(log_decay):
    span = log_decay.shape[0]
    lower = (iota((span, span), 0) >= iota((span, span), 1)).astype(bf16)
    return folded(mm(lower, halves(log_decay)))


def decay_matrix(running, running_rows, head):
    span = running.shape[0]
    at = 64 * head
    spread = running[:, at : at + 1] - running_rows[at : at + 1, :]
    return jnp.exp(jnp.where(iota((span, span), 0) >= iota((span, span), 1), spread, -jnp.inf))


def forward_kernel(
    stream_ref, edge_ref, step_ref, taps_ref, bias_ref, step_bias_ref, rate_ref, skip_ref,
    mixed_out, active_out, slope_out, reach_out, steps_out, states_out,
    ext, state, offset,
):
    span = SPAN
    first = pl.program_id(0) == 0

    @pl.when(first)
    def _():
        ext[0:8] = edge_ref[...].astype(f32)
        state[...] = jnp.zeros_like(state)
        offset[...] = jnp.zeros_like(offset)

    ext[8 : 8 + span] = stream_ref[...].astype(f32)
    conv = convolved(ext, taps_ref[...], bias_ref[...])
    ext[0:8] = ext[span : span + 8]
    chance = logistic(conv)
    active = conv * chance
    active_out[...] = active
    slope_out[...] = chance * (1.0 + conv * (1.0 - chance))
    values = active[:, 0:128]
    keys = active[:, 128:256]
    queries = active[:, 256:384]
    step = step_ref[...] + step_bias_ref[...]
    widths = softplus(step)
    running = running_sums(-rate_ref[...] * widths)
    steps_out[:, 0:128] = widths
    steps_out[:, 128:256] = running
    steps_out[:, 256:384] = logistic(step)
    running_rows = running.T
    last = running[span - 1 : span, :]
    fed = widths * values
    fed16 = fed.astype(bf16)
    query_terms = left_terms(queries, 1)
    scores = mm_nt(queries.astype(bf16), keys.astype(bf16))
    low = iota((span, 128), 1) < 64
    heads = [
        mm((scores * decay_matrix(running, running_rows, head)).astype(bf16), fed16)
        for head in range(2)
    ]
    before = state[...]
    mixed = jnp.where(low, heads[0], heads[1])
    mixed = mixed + jnp.exp(running) * mm_nt(query_terms, wide_terms(before))
    mixed_out[...] = mixed + skip_ref[...] * values
    reach_out[...] = running + offset[0:1]
    offset[...] = offset[...] + last
    tails = left_terms(jnp.exp(last - running) * fed, 0)
    after = jnp.exp(running_rows[:, span - 1 : span]) * before + mm_tn(tails, right_terms(keys))
    state[...] = after
    states_out[0] = after


def scan_forward(stream, edge, step, taps, bias, step_bias, rate, skip):
    rows = stream.shape[0]
    span = SPAN
    count = rows // span
    row = lambda i: (i, 0)
    narrow, full = spec((span, 128), row), spec((span, 384), row)
    return pl.pallas_call(
        forward_kernel,
        grid=(count,),
        in_specs=[
            full, whole_block(edge), narrow, whole_block(taps), whole_block(bias),
            whole_block(step_bias), whole_block(rate), whole_block(skip),
        ],
        out_specs=[
            narrow, full, full, narrow, full, spec((1, 128, 128), lambda i: (i, 0, 0)),
        ],
        out_shape=[
            jax.ShapeDtypeStruct((rows, 128), f32),
            jax.ShapeDtypeStruct((rows, 384), f32),
            jax.ShapeDtypeStruct((rows, 384), f32),
            jax.ShapeDtypeStruct((rows, 128), f32),
            jax.ShapeDtypeStruct((rows, 384), f32),
            jax.ShapeDtypeStruct((count, 128, 128), f32),
        ],
        scratch_shapes=[
            pltpu.VMEM((span + 8, 384), f32), pltpu.VMEM((128, 128), f32), pltpu.VMEM((8, 128), f32),
        ],
        compiler_params=params(56),
        cost_estimate=pl.CostEstimate(
            flops=count * 2 * span * span * 900, bytes_accessed=rows * 128 * 50, transcendentals=0
        ),
    )(stream, edge, step, taps, bias, step_bias, rate, skip)


def join_kernel(
    mixed_ref, query_ref, reach_ref, gate_ref, grad_ref, carried_ref, gain_ref, mixed_out, sums_out
):
    inner = mm_nt(left_terms(query_ref[...], 1), wide_terms(carried_ref[...]))
    mixed = mixed_ref[...] + jnp.exp(reach_ref[...]) * inner
    mixed_out[...] = mixed
    gate = gate_ref[...]
    gated = mixed * (gate * logistic(gate))
    at = 2 * pl.program_id(0)
    sums_out[pl.ds(at, 1), :] = jnp.sum((gated * gated).T, axis=0, keepdims=True)
    product = grad_ref[...] * gain_ref[...] * gated
    sums_out[pl.ds(at + 1, 1), :] = jnp.sum(product.T, axis=0, keepdims=True)


def join(mixed, active, reach, gate, grad, carried, gain):
    rows = mixed.shape[0]
    block = 1024
    sums = (2 * rows // block, block)
    blocks = spec((block, 128), lambda i: (i, 0))
    return pl.pallas_call(
        join_kernel,
        grid=(rows // block,),
        in_specs=[
            blocks, spec((block, 128), lambda i: (i, 2)), blocks, blocks, blocks,
            whole_block(carried), whole_block(gain),
        ],
        out_specs=[blocks, spec(sums, lambda i: (0, 0))],
        out_shape=[jax.ShapeDtypeStruct((rows, 128), f32), jax.ShapeDtypeStruct(sums, f32)],
        compiler_params=params(56),
        cost_estimate=pl.CostEstimate(
            flops=2 * rows * 128 * 128, bytes_accessed=rows * 128 * 22, transcendentals=0
        ),
    )(mixed, active, reach, gate, grad, carried, gain)


def gate_kernel(
    inner_width,
    mixed_ref, query_ref, reach_ref, gate_ref, grad_ref, sums_ref, gain_ref,
    rows_out, gate_out, mixed_grad_out, gain_out, incoming_out,
):
    @pl.when(pl.program_id(0) == 0)
    def _():
        gain_out[...] = jnp.zeros_like(gain_out)
        incoming_out[...] = jnp.zeros_like(incoming_out)

    block = mixed_ref.shape[0]
    at = 2 * pl.program_id(0)
    square = jnp.broadcast_to(sums_ref[pl.ds(at, 1), :], (128, block)).T
    product = jnp.broadcast_to(sums_ref[pl.ds(at + 1, 1), :], (128, block)).T
    scale = lax.rsqrt(square / inner_width + epsilon)
    gate = gate_ref[...]
    chance = logistic(gate)
    act = gate * chance
    mixed = mixed_ref[...]
    hat = mixed * act * scale
    rows_out[...] = (hat * gain_ref[...]).astype(bf16)
    grad = grad_ref[...]
    gain_out[...] += jnp.sum(grad * hat, axis=0, keepdims=True)
    pre = scale * (grad * gain_ref[...] - hat * (product * scale / inner_width))
    mixed_grad = pre * act
    mixed_grad_out[...] = mixed_grad
    gate_out[...] = (pre * mixed * (chance * (1.0 + gate * (1.0 - chance)))).astype(bf16)
    incoming_out[...] += mm_tn(
        left_terms(jnp.exp(reach_ref[...]) * mixed_grad, 0), right_terms(query_ref[...])
    )


def gate_step(mixed, active, reach, gate, grad, sums, gain, inner_width):
    rows = mixed.shape[0]
    block = sums.shape[1]
    blocks = spec((block, 128), lambda i: (i, 0))
    return pl.pallas_call(
        partial(gate_kernel, inner_width),
        grid=(rows // block,),
        in_specs=[
            blocks, spec((block, 128), lambda i: (i, 2)), blocks, blocks, blocks, whole_block(sums),
            whole_block(gain),
        ],
        out_specs=[
            blocks, blocks, blocks, spec((1, 128), lambda i: (0, 0)),
            spec((128, 128), lambda i: (0, 0)),
        ],
        out_shape=[
            jax.ShapeDtypeStruct((rows, 128), bf16),
            jax.ShapeDtypeStruct((rows, 128), bf16),
            jax.ShapeDtypeStruct((rows, 128), f32),
            jax.ShapeDtypeStruct((1, 128), f32),
            jax.ShapeDtypeStruct((128, 128), f32),
        ],
        compiler_params=params(56),
        cost_estimate=pl.CostEstimate(
            flops=2 * rows * 128 * 128, bytes_accessed=rows * 128 * 26, transcendentals=0
        ),
    )(mixed, active, reach, gate, grad, sums, gain)


def head_sums(x):
    same = (iota((128, 128), 0) < 64) == (iota((128, 128), 1) < 64)
    ones = same.astype(bf16)
    high = x.astype(bf16)
    return mm(high, ones) + mm((x - high.astype(f32)).astype(bf16), ones)


def backward_kernel(
    first_chunk,
    stream_ref, before_ref, edge_ref, active_ref, slope_ref, steps_ref, taps_ref, rate_ref, skip_ref,
    mixed_ref, grad_ref, reach_ref, start_ref, end_ref, carried_ref, arriving_ref, next_ref,
    stream_grad_out, tail_out, head_out, sums_out, leaving_out,
    ext, grads, state_grad,
):
    span = SPAN
    chunk = first_chunk - pl.program_id(0)

    @pl.when(pl.program_id(0) == 0)
    def _():
        state_grad[...] = arriving_ref[...]
        grads[span : span + 8] = next_ref[...]
        sums_out[...] = jnp.zeros_like(sums_out)

    @pl.when(chunk == 0)
    def _():
        ext[0:8] = edge_ref[...].astype(f32)

    @pl.when(chunk > 0)
    def _():
        ext[0:8] = before_ref[8:16].astype(f32)

    ext[8 : 8 + span] = stream_ref[...].astype(f32)
    taps = taps_ref[...]
    values = active_ref[:, 0:128]
    keys = active_ref[:, 128:256]
    queries = active_ref[:, 256:384]
    keys16 = keys.astype(bf16)
    rate = rate_ref[...]
    widths = steps_ref[:, 0:128]
    running = steps_ref[:, 128:256]
    running_rows = running.T
    last = running[span - 1 : span, :]
    fed = widths * values
    fed16 = fed.astype(bf16)
    grad = grad_ref[...]
    grad16 = grad.astype(bf16)
    scores = mm_nt(queries.astype(bf16), keys16)
    low = iota((span, 128), 1) < 64
    grad_turned = pltpu.roll(grad, 64, 1)
    fed_turned = pltpu.roll(fed, 64, 1)
    score_grad = None
    fed_grads = []
    for head in range(2):
        decay = decay_matrix(running, running_rows, head)
        mine = low == (head == 0)
        grad_high, grad_low = two(jnp.where(mine, grad, grad_turned))
        left = [jnp.where(low, grad_high, grad_low), jnp.where(low, grad_high, 0)]
        right = two(jnp.where(mine, fed, fed_turned))
        part = mm_nt(jnp.concatenate(left, axis=1), jnp.concatenate(right, axis=1)) * decay
        score_grad = part if score_grad is None else score_grad + part
        fed_grads.append(mm_tn((scores * decay).astype(bf16), grad16))

    offset = (reach_ref[span - 8 : span, :] - running[span - 8 : span, :]).T[:, 7:8]
    carried = jnp.exp(offset) * carried_ref[...]
    before = jnp.where(chunk > 0, start_ref[0], 0.0) + carried
    last_rows = jnp.exp(running_rows[:, span - 1 : span])
    after = end_ref[0] + last_rows * carried
    after_grad = state_grad[...]
    tail = jnp.exp(last - running)
    reached = jnp.exp(running) * grad
    query_terms = right_terms(queries)
    fed_grad = jnp.where(low, fed_grads[0], fed_grads[1])
    fed_grad = fed_grad + tail * mm_nt(keys16, after_grad.astype(bf16))
    score_high, score_low = two(score_grad)
    query_grad = mm(
        jnp.concatenate([score_high, score_high, score_low], axis=1), right_terms(keys)
    ) + mm(left_terms(reached, 1), right_terms(before))
    key_grad = mm_tn(
        jnp.concatenate([score_high, score_high, score_low], axis=0), query_terms
    ) + mm(left_terms(tail * fed, 1), right_terms(after_grad))
    leaving = last_rows * after_grad + mm_tn(left_terms(reached, 0), query_terms)
    state_grad[...] = leaving
    leaving_out[...] = leaving
    value_grad = widths * fed_grad + skip_ref[...] * grad

    mixed = mixed_ref[...] - skip_ref[...] * values
    balance = head_sums(grad16.astype(f32) * mixed - fed16.astype(f32) * fed_grad)
    upper = (iota((span, span), 0) <= iota((span, span), 1)).astype(bf16)
    boundary = head_sums(
        jnp.broadcast_to(jnp.sum((after_grad * after).T, axis=0, keepdims=True), (8, 128))
    )
    decay_grad = folded(mm(upper, halves(balance))) + boundary[0:1]
    width_grad = head_sums(values * fed_grad) - rate * decay_grad
    step_grad = width_grad * steps_ref[:, 256:384]
    sums_out[0:1, 384:512] += jnp.sum(step_grad, axis=0, keepdims=True)
    sums_out[1:2, 384:512] += jnp.sum(-widths * decay_grad, axis=0, keepdims=True)
    sums_out[2:3, 384:512] += jnp.sum(grad * values, axis=0, keepdims=True)

    conv_grad = jnp.concatenate([value_grad, key_grad, query_grad], axis=1) * slope_ref[...]
    grads[0:span] = conv_grad
    for tap in range(4):
        sums_out[tap : tap + 1, 0:384] += jnp.sum(
            conv_grad * ext[5 + tap : 5 + tap + span], axis=0, keepdims=True
        )
    sums_out[4:5, 0:384] += jnp.sum(conv_grad, axis=0, keepdims=True)
    stream_grad = taps[3:4] * conv_grad
    for tap in range(3):
        stream_grad = stream_grad + taps[tap : tap + 1] * grads[3 - tap : 3 - tap + span]
    high = stream_grad.astype(bf16)
    stream_grad_out[:, 0:384] = high
    stream_grad_out[:, 384:512] = step_grad.astype(bf16)
    stream_grad_out[:, 512:768] = (stream_grad - high.astype(f32))[:, 128:384].astype(bf16)

    @pl.when(pl.program_id(0) == 0)
    def _():
        tail_out[...] = stream_grad[span - 8 :]

    head_out[...] = conv_grad[0:8]
    grads[span : span + 8] = conv_grad[0:8]


def scan_backward(
    late, stream, edge, active, slope, steps, taps, rate, skip, mixed, grad, reach, states, carried,
    arriving, next_rows,
):
    rows = stream.shape[0]
    span = SPAN
    early = rows // span // 4
    count = 3 * early if late else early
    first = 4 * early - 1 if late else early - 1
    row = lambda i: (first - i, 0)
    fixed = lambda i: (0, 0)
    narrow, full = spec((span, 128), row), spec((span, 384), row)
    return pl.pallas_call(
        partial(backward_kernel, first),
        grid=(count,),
        in_specs=[
            full, spec((16, 384), lambda i: (jnp.maximum((first - i) * (span // 16) - 1, 0), 0)),
            whole_block(edge), full, full, full, whole_block(taps), whole_block(rate),
            whole_block(skip), narrow, narrow, narrow,
            spec((1, 128, 128), lambda i: (jnp.maximum(first - 1 - i, 0), 0, 0)),
            spec((1, 128, 128), lambda i: (first - i, 0, 0)),
            whole_block(carried), whole_block(arriving), whole_block(next_rows),
        ],
        out_specs=[
            spec((span, 768), lambda i: (count - 1 - i, 0)), spec((8, 384), fixed),
            spec((8, 384), fixed), spec((8, 512), fixed), spec((128, 128), fixed),
        ],
        out_shape=[
            jax.ShapeDtypeStruct((count * span, 768), bf16),
            jax.ShapeDtypeStruct((8, 384), f32),
            jax.ShapeDtypeStruct((8, 384), f32),
            jax.ShapeDtypeStruct((8, 512), f32),
            jax.ShapeDtypeStruct((128, 128), f32),
        ],
        scratch_shapes=[
            pltpu.VMEM((span + 8, 384), f32), pltpu.VMEM((span + 8, 384), f32),
            pltpu.VMEM((128, 128), f32),
        ],
        compiler_params=params(56),
        cost_estimate=pl.CostEstimate(
            flops=count * 2 * span * span * 1500, bytes_accessed=rows * 128 * 30, transcendentals=0
        ),
    )(
        stream, stream, edge, active, slope, steps, taps, rate, skip, mixed, grad, reach, states,
        states, carried, arriving, next_rows,
    )


def group_of(rows, index):
    early = rows // BLOCK // 4
    late = 3 * early - 1
    if index == 0:
        return late, lambda place: early + place
    return early + 1, lambda place: jnp.where(place < early, place, place + late)


def parts_kernel(
    block_of, last_block, early_blocks,
    place_ref, gate_ref, early_ref, late_ref, weights_ref, hidden_ref, scale_ref, gain_ref, tail_ref,
    next_ref, taps_ref,
    own_out, other_out, dots_out, sums_out,
    left, edge,
):
    at_block = block_of(pl.program_id(0))

    @pl.when(pl.program_id(0) == 0)
    def _():
        sums_out[...] = jnp.zeros_like(sums_out)

    block = left.shape[0]
    left[:, 0:128] = gate_ref[...]

    @pl.when(at_block < early_blocks)
    def _():
        left[:, 128:640] = early_ref[...]

    @pl.when(at_block >= early_blocks)
    def _():
        left[:, 128:640] = late_ref[...]

    @pl.when(at_block == last_block)
    def _():
        edge[0:8] = jnp.zeros_like(edge[0:8])
        edge[8:16] = next_ref[...]
        fixed = tail_ref[...]
        for tap in range(3):
            fixed = fixed + taps_ref[tap : tap + 1] * edge[3 - tap : 11 - tap]
        left[block - 8 :, 128:512] = fixed.astype(bf16)

    chips, share, _ = own_out.shape
    total = mm(left[...], weights_ref[...]).astype(bf16)
    scale = scale_ref[...]
    summed = None
    turned = []
    for at in range(0, total.shape[1], 128):
        lanes = slice(at, at + 128)
        part = total[:, lanes].astype(f32)
        turned.append(part.T)
        product = part * (hidden_ref[:, lanes].astype(f32) * scale)
        sums_out[0:1, lanes] += jnp.sum(product, axis=0, keepdims=True)
        product = product * gain_ref[:, lanes]
        summed = product if summed is None else summed + product
    dots_out[...] = jnp.sum(summed.T, axis=0, keepdims=True)
    turned = jnp.concatenate(turned, axis=0)
    second = place_ref[1] == 1
    for chip in range(chips):
        low = turned[2 * chip * share : (2 * chip + 1) * share]
        high = turned[(2 * chip + 1) * share : (2 * chip + 2) * share]
        own_out[chip] = jnp.where(second, high, low).astype(bf16)
        other_out[chip] = jnp.where(second, low, high).astype(bf16)


def input_parts(
    index, place, gate16, early16, late16, weights, hidden_in, scale, gain, tail, next_head, taps,
    chips,
):
    rows, width = hidden_in.shape
    block = BLOCK
    count, block_of = group_of(rows, index)
    blocks = rows // block
    row = lambda i, at: (block_of(i), 0)
    share = width // chips // 2
    turned = spec((chips, share, block), lambda i, at: (0, 0, i))
    return pl.pallas_call(
        partial(parts_kernel, block_of, blocks - 1, blocks // 4),
        grid_spec=pltpu.PrefetchScalarGridSpec(
            num_scalar_prefetch=1,
            grid=(count,),
            in_specs=[
                spec((block, 128), row),
                spec((block, 512), lambda i, at: (jnp.minimum(block_of(i), blocks // 4 - 1), 0)),
                spec((block, 512), lambda i, at: (jnp.maximum(block_of(i) - blocks // 4, 0), 0)),
                whole_block(weights), spec((block, width), row), spec((block, 128), row),
                whole_block(gain), whole_block(tail), whole_block(next_head), whole_block(taps),
            ],
            out_specs=[
                turned, turned, spec((1, block), lambda i, at: (0, i)),
                spec((1, width), lambda i, at: (0, 0)),
            ],
            scratch_shapes=[pltpu.VMEM((block, 640), bf16), pltpu.VMEM((16, 384), f32)],
        ),
        out_shape=[
            jax.ShapeDtypeStruct((chips, share, count * block), bf16),
            jax.ShapeDtypeStruct((chips, share, count * block), bf16),
            jax.ShapeDtypeStruct((1, count * block), f32),
            jax.ShapeDtypeStruct((1, width), f32),
        ],
        compiler_params=params(56),
        cost_estimate=pl.CostEstimate(
            flops=2 * count * block * width * 640, bytes_accessed=count * block * width * 5,
            transcendentals=0,
        ),
    )(
        place, gate16, early16, late16, weights, hidden_in, scale, gain, tail, next_head, taps
    )


def output_kernel(at_ref, rows_ref, weights_ref, hidden_ref, parts_out):
    groups, share, _ = parts_out.shape
    summed = None
    for group in range(rows_ref.shape[0]):
        term = mm(rows_ref[group], weights_ref[group]).astype(bf16).astype(f32)
        summed = term if summed is None else summed + term
    total = hidden_ref[...].astype(f32) + summed
    turned = [total[:, at : at + 128].T for at in range(0, total.shape[1], 128)]
    turned = jnp.concatenate(turned, axis=0)
    for group in range(groups):
        parts_out[group] = turned[group * share : (group + 1) * share].astype(bf16)


def output_rows(rows, weights, hidden, at):
    groups, tokens, inner = rows.shape
    width = hidden.shape[1]
    block = min(tokens, SPAN)
    steps = tokens // block
    share = width // groups
    return pl.pallas_call(
        output_kernel,
        grid_spec=pltpu.PrefetchScalarGridSpec(
            num_scalar_prefetch=1,
            grid=(steps,),
            in_specs=[
                spec((groups, block, inner), lambda i, at: (0, i, 0)), whole_block(weights),
                spec((block, width), lambda i, at: (steps * at[0] + i, 0)),
            ],
            out_specs=spec((groups, share, block), lambda i, at: (0, 0, i)),
        ),
        out_shape=jax.ShapeDtypeStruct((groups, share, tokens), bf16),
        compiler_params=params(56),
        cost_estimate=pl.CostEstimate(
            flops=2 * tokens * groups * inner * width, bytes_accessed=8 << 20, transcendentals=0
        ),
    )(at, rows, weights, hidden)


def side_kernel(blocks_ref, out_ref):
    tokens = blocks_ref.shape[2]
    for at in range(blocks_ref.shape[0]):
        out_ref[:, at * tokens : (at + 1) * tokens] = blocks_ref[at]


def side_by_side(blocks):
    count, share, tokens = blocks.shape
    return pl.pallas_call(
        side_kernel,
        grid=(count // 2,),
        in_specs=[spec((2, share, tokens), lambda i: (i, 0, 0))],
        out_specs=spec((share, 2 * tokens), lambda i: (0, i)),
        out_shape=jax.ShapeDtypeStruct((share, count * tokens), blocks.dtype),
        compiler_params=params(56),
    )(blocks)


def row_major(x):
    return with_layout_constraint(x, Layout(major_to_minor=(0, 1)))


def passed_along(block, axis, distance):
    devices = range(lax.axis_size(axis))
    route = [(i - distance, i) for i in devices if i - distance in devices]
    return lax.ppermute(block, axis, route)


def bits_of(axis):
    count = lax.axis_size(axis)
    assert count & (count - 1) == 0
    return [1 << n for n in range(count.bit_length() - 1)]


def summed_over(value, axis, turned=False, bits=None, dtype=f32):
    count = lax.axis_size(axis)
    bits = bits_of(axis) if bits is None else bits
    for bit in reversed(bits) if turned else bits:
        value = value.astype(dtype)
        sent = lax.ppermute(value, axis, [(i, i ^ bit) for i in range(count)])
        value = value.astype(f32) + sent.astype(f32)
    return value


def spread_sums(pair, axis):
    chips = pair.shape[0]
    mine = lax.axis_index(axis)
    spread = jnp.stack([pair, jnp.zeros_like(pair)], axis=1)
    spread = jnp.where(mine % 2 == 0, spread, spread[:, ::-1])
    spread = spread.reshape(2 * chips, *pair.shape[1:])
    return lax.psum_scatter(spread, axis, scatter_dimension=0, tiled=False).astype(f32)


def line_kernel(at_ref, up_own, up_got, down_own, down_got, *refs):
    up_out, down_out = refs[-2:]
    up = up_own[0].astype(f32) + up_got[0].astype(f32)
    down = down_own[0].astype(f32) + down_got[0].astype(f32)
    if len(refs) == 4:
        up, down = up + refs[0][...].astype(f32), down + refs[1][...].astype(f32)
    up_out[...] = up.astype(bf16)
    down_out[...] = down.astype(bf16)


def line_step(up_at, down_at, own, got, arrived):
    chips, share, tokens = own.shape
    block = tokens // 2
    at = jnp.stack([up_at, down_at]).astype(jnp.int32)
    at = jnp.clip(at, 0, chips - 1)
    blocks = [spec((1, share, block), lambda i, at, k=k: (at[k], 0, i)) for k in (0, 0, 1, 1)]
    plain = spec((share, block), lambda i, at: (0, i))
    return pl.pallas_call(
        line_kernel,
        grid_spec=pltpu.PrefetchScalarGridSpec(
            num_scalar_prefetch=1,
            grid=(2,),
            in_specs=blocks + [plain] * len(arrived),
            out_specs=[plain, plain],
        ),
        out_shape=[jax.ShapeDtypeStruct((share, tokens), bf16)] * 2,
        compiler_params=params(56),
        cost_estimate=pl.CostEstimate(
            flops=share * tokens * 4, bytes_accessed=share * tokens * 16, transcendentals=0
        ),
    )(at, own, got, own, got, *arrived)


def line_sent(step, sent, axis):
    chips, cores = 4, 2
    last = chips * cores - 1
    up = lax.ppermute(sent[0], axis, [(i, i + cores) for i in range(cores * step)])
    down_route = [(last - i, last - i - cores) for i in range(cores * step)]
    down = lax.ppermute(sent[1], axis, down_route)
    return up, down


def line_terms(step, own, got, arrived, axis):
    chip = lax.axis_index(axis) // 2
    return line_step(4 + chip - step, step - 4 + chip, own, got, arrived)


after = lax.optimization_barrier


def own_features(rows, second):
    share = rows.shape[1] // 2
    turned = [rows[:, at : at + 128].T for at in range(0, 2 * share, 128)]
    turned = jnp.concatenate(turned, axis=0)
    return jnp.where(second, turned[share:], turned[:share])


def finish_kernel(
    width,
    place_ref, own_ref, got_ref, up_ref, down_ref, hidden_ref, scale_ref, gain_ref, dots_ref,
    grad_ref, *refs,
):
    out_ref = refs[-1]
    second = place_ref[1] == 1
    total = own_ref[0].astype(f32) + got_ref[0].astype(f32)
    total = total + up_ref[...].astype(f32) + down_ref[...].astype(f32)
    gain = jnp.broadcast_to(gain_ref[...], (8, gain_ref.shape[1]))
    gain = own_features(gain, second)[:, 0:1]
    scale = scale_ref[...]
    dot = dots_ref[...] * (1.0 / width) * (scale * scale)
    normal = own_features(hidden_ref[...].astype(f32), second)
    base = own_features(grad_ref[...].astype(f32), second) - normal * dot
    out_ref[...] = base + total * (gain * scale)


def finish(index, own, got, up, down, hidden_in, scale, gain, dots, out_grad, place, target):
    rows, width = hidden_in.shape
    share = own.shape[1]
    both = 2 * share
    block = BLOCK
    count, block_of = group_of(rows, index)
    here = spec((1, share, block), lambda i, at: (at[0], 0, i))
    plain = spec((share, block), lambda i, at: (0, i))
    feature = spec((block, both), lambda i, at: (block_of(i), at[0]))
    operands = [place, own, got, up, down, hidden_in, scale, gain, dots, out_grad]
    in_specs = [
        here, here, plain, plain, feature, spec((1, block), lambda i, at: (0, block_of(i))),
        spec((1, both), lambda i, at: (0, at[0])), spec((1, block), lambda i, at: (0, i)), feature,
    ]
    aliases = {}
    if target is not None:
        aliases = {len(operands): 0}
        operands.append(target)
        in_specs.append(pl.BlockSpec(memory_space=pl.ANY))
    return pl.pallas_call(
        partial(finish_kernel, width),
        grid_spec=pltpu.PrefetchScalarGridSpec(
            num_scalar_prefetch=1,
            grid=(count,),
            in_specs=in_specs,
            out_specs=spec((share, block), lambda i, at: (0, block_of(i))),
        ),
        out_shape=jax.ShapeDtypeStruct((share, rows), f32),
        input_output_aliases=aliases,
        compiler_params=params(56),
        cost_estimate=pl.CostEstimate(
            flops=rows * both * 5, bytes_accessed=count * block * both * 12, transcendentals=0
        ),
    )(*operands)


def chained(states, decays, mine, backward):
    count = states.shape[0]
    order = range(count)
    if backward:
        order = reversed(order)
    total = jnp.zeros_like(states[0])
    for at in order:
        use = at > mine if backward else at < mine
        total = jnp.where(use, decays[at][:, None] * total + states[at], total)
    return total


def block(
    hidden_in, norm_gain, gate_proj, value_proj, state_proj, step_proj, conv_value,
    conv_value_bias, conv_state, conv_state_bias, step_bias, decay_rate, skip_gain, mix_gain,
    out_proj, out_grad,
):
    rows, width = hidden_in.shape
    groups = lax.axis_size("head")
    share = width // groups
    mine = lax.axis_index("head")
    first_col = mine * share
    chips = groups // 2
    core = mine % 2
    inner_local = gate_proj.shape[1]
    inner_width = inner_local * groups
    heads = step_proj.shape[1]
    head_size = inner_local // heads

    def wide(x):
        return jnp.repeat(x, head_size, axis=-1)

    step_wide = wide(step_proj)
    rate, skip, step_shift = (wide(x)[None, :] for x in (decay_rate, skip_gain, step_bias))
    taps = jnp.concatenate([conv_value, conv_state], axis=1)
    bias = jnp.concatenate([conv_value_bias, conv_state_bias])[None, :]
    gain = mix_gain[None, :]

    all_out_proj = lax.all_gather(out_proj, "head")
    projected, gate_in, stream, step, scale_in, scale_row = project(
        hidden_in, norm_gain, gate_proj, value_proj, state_proj, step_wide
    )
    edge = passed_along(stream[rows - 8 :], "seq", 1)
    grad_gated = lax.dot_general(
        out_grad, out_proj, (((1,), (1,)), ((), ())), preferred_element_type=f32
    )
    partial_mixed, active, slope, reach, steps, states = scan_forward(
        stream, edge, step, taps, bias, step_shift, rate, skip
    )
    at_seq = lax.axis_index("seq")
    decay_here = jnp.exp(reach[rows - 1])
    packed = jnp.concatenate([states[-1], jnp.broadcast_to(decay_here[None, :], (8, 128))])
    gathered = lax.all_gather(packed, "seq")
    decays = gathered[:, 128]
    carried = chained(gathered[:, :128], decays, at_seq, False)
    mixed, sums = join(partial_mixed, active, reach, gate_in, grad_gated, carried, gain)
    sums = summed_over(sums, "head", False)
    gated_rows, grad_gate16, grad_mixed, grad_mix_gain, incoming = gate_step(
        mixed, active, reach, gate_in, grad_gated, sums, gain, inner_width
    )

    own_tokens = rows // groups
    group_rows = lax.all_to_all(
        gated_rows.reshape(groups, own_tokens, inner_local), "head", 0, 0, tiled=False
    )
    on_line = chips == 4 and 2 * share % 128 == 0
    partner = [(i, i ^ 1) for i in range(groups)]
    place = jnp.stack([mine // 2, core]).astype(jnp.int32)
    arriving = chained(lax.all_gather(incoming, "seq"), decays, at_seq, True)
    scan_args = (
        stream, edge, active, slope, steps, taps, rate, skip, mixed, grad_mixed, reach, states, carried
    )
    late16, tail, head, late_sums, arriving = scan_backward(
        True, *scan_args, arriving, jnp.zeros((8, stream.shape[1]), f32)
    )
    step_back = wide(step_proj).T * (1.0 / head_size)
    weights = jnp.concatenate(
        [gate_proj.T, value_proj.T, state_proj.T, step_back.astype(bf16)], axis=0
    )
    gain_in = norm_gain[None, :]

    def parts_of(index, early16, next_head):
        return input_parts(
            index, place, grad_gate16, early16, late16, weights, hidden_in, scale_in, gain_in, tail,
            next_head, taps, chips,
        )

    group_rows, late16 = after((group_rows, late16))
    out_parts = output_rows(group_rows, all_out_proj, hidden_in, mine.astype(jnp.int32)[None])
    out_parts = lax.all_to_all(out_parts, "head", 0, 0, tiled=False)
    own_0, other_0, dots_0, norm_sums = parts_of(0, late16, head)
    got_0 = lax.ppermute(other_0, "head", partner)
    early16, _, head, early_sums, _ = scan_backward(False, *scan_args, arriving, head)
    next_head = passed_along(head, "seq", -1)
    if on_line:
        line_0 = line_terms(1, own_0, got_0, (), "head")
        line_0 = line_sent(1, line_0, "head")
    contract = (((0,), (0,)), ((), ()))

    def product(left, right):
        return lax.dot_general(left, right, contract, preferred_element_type=f32)

    own_1, other_1, dots_1, more_sums = parts_of(1, early16, next_head)
    norm_sums = norm_sums + more_sums
    got_1 = lax.ppermute(other_1, "head", partner)
    grad_out_proj = product(gated_rows, out_grad)
    dots = jnp.concatenate([dots_0.reshape(-1, 128), dots_1.reshape(-1, 128)], axis=0)
    needs = (late16, next_head, projected)
    if on_line:
        sent = line_terms(1, own_1, got_1, (), "head")
        sent, needs, dots = after((sent, needs, dots))
        line_1 = line_sent(1, sent, "head")
        line_0 = line_terms(2, own_0, got_0, line_0, "head")
        line_0 = line_sent(2, line_0, "head")
    sums = (late_sums + early_sums).at[5, :128].set(grad_mix_gain[0])
    headed = jnp.concatenate(
        [sums[:5, 128:384].reshape(-1, 128), norm_sums.reshape(-1, 128), dots], axis=0
    )
    head_bits, seq_bits = bits_of("head"), bits_of("seq")
    headed = summed_over(headed, "head", False, head_bits[:2])
    grad_out_proj = summed_over(grad_out_proj, "seq", False, seq_bits[:1], bf16)

    late_fixed, next_rows, projected = needs
    extra = [sum(taps[tap] * next_rows[row - tap] for tap in range(row + 1)) for row in range(3)]
    fixed = tail.at[5:].add(jnp.stack(extra))
    fixed16 = fixed.astype(bf16)
    low16 = (fixed - fixed16.astype(f32))[:, inner_local:].astype(bf16)
    late_fixed = lax.dynamic_update_slice(late_fixed, fixed16, (rows - rows // 4 - 8, 0))
    late_fixed = lax.dynamic_update_slice(late_fixed, low16, (rows - rows // 4 - 8, 512))
    rest16 = jnp.concatenate([early16, late_fixed], axis=0)
    grad_rest = product(projected, rest16)
    state_part = row_major(grad_rest[:, 128:384] + grad_rest[:, 512:768])
    if on_line:
        line_1, state_part = after((line_1, state_part))
        sent = line_terms(2, own_1, got_1, line_1, "head")
        sent, headed = after((sent, headed))
        line_1 = line_sent(2, sent, "head")
        sent = line_terms(3, own_0, got_0, line_0, "head")
        sent, projected, sums, grad_rest, grad_out_proj = after(
            (sent, projected, sums, grad_rest, grad_out_proj)
        )
        line_0 = line_sent(3, sent, "head")
    headed = summed_over(headed, "head", False, head_bits[2:])
    unit_dot, headed = headed[-dots.shape[0] :], headed[: -dots.shape[0]]
    grad_value_proj = row_major(grad_rest[:, :128])
    step_sums = row_major(grad_rest[:, 384:512]).T[::head_size]
    grad_gate_proj = row_major(product(projected, grad_gate16))
    grad_state_proj = lax.psum_scatter(state_part, "head", scatter_dimension=0, tiled=True)
    grad_state_proj = summed_over(grad_state_proj, "seq", False)
    grad_value_proj = summed_over(grad_value_proj, "seq", False, None, bf16)
    grad_gate_proj = summed_over(grad_gate_proj, "seq", True, None, bf16)
    grad_out_proj = summed_over(grad_out_proj, "seq", False, seq_bits[1:], bf16)

    small = jnp.concatenate(
        [sums.reshape(-1, 128), step_sums.reshape(-1, 128), headed.reshape(-1, 128)], axis=0
    )
    small = summed_over(small, "seq", False).reshape(-1)
    at = sums.size
    sums, small = small[:at].reshape(8, 512), small[at:]
    grad_step_proj, small = small[: heads * width].reshape(heads, width).T, small[heads * width :]
    state_sums, norm_sums = small[: 5 * 256].reshape(5, 256), small[5 * 256 :]
    grad_norm_gain = lax.dynamic_slice_in_dim(norm_sums, first_col, share, 0)
    unit_dot = unit_dot.reshape(1, -1)
    dots_0, dots_1 = unit_dot[:, : dots_0.size], unit_dot[:, dots_0.size :]

    if on_line:
        sent = line_terms(3, own_1, got_1, line_1, "head")
        sent, own_0, out_parts = after((sent, own_0, out_parts))
        line_1 = line_sent(3, sent, "head")
    block_out = side_by_side(out_parts).T
    if on_line:
        grad_input = None
        for index, own, got, (up, down), dots in (
            (0, own_0, got_0, line_0, dots_0), (1, own_1, got_1, line_1, dots_1)
        ):
            grad_input = finish(
                index, own, got, up, down, hidden_in, scale_row, gain_in, dots, out_grad, place,
                grad_input,
            )
        grad_input = grad_input.T
    else:
        pieces = []
        for own, got in ((own_0, got_0), (own_1, got_1)):
            pair = (own.astype(f32) + got.astype(f32)).astype(bf16)
            pieces.append(spread_sums(pair, "head").T)
        cut = rows // 4
        grad_projected = jnp.concatenate([pieces[1][:cut], pieces[0], pieces[1][cut:]])
        dots_0, dots_1 = dots_0.reshape(-1), dots_1.reshape(-1)
        unit_dot = jnp.concatenate([dots_1[:cut], dots_0, dots_1[cut:]])
        hidden_own = lax.dynamic_slice_in_dim(hidden_in, first_col, share, 1).astype(f32)
        gain_own = lax.dynamic_slice_in_dim(norm_gain, first_col, share, 0)
        scale_col = scale_in[:, :1]
        normal_own = hidden_own * scale_col
        grad_unit = grad_projected * gain_own[None, :]
        grad_input = scale_col * (grad_unit - normal_own * (unit_dot / width)[:, None])
        out_grad_own = lax.dynamic_slice_in_dim(out_grad, first_col, share, 1)
        grad_input = grad_input + out_grad_own.astype(f32)

    head_rows = sums[:3, 384:512].reshape(3, heads, head_size)
    return (
        block_out,
        grad_input,
        grad_norm_gain,
        grad_gate_proj,
        grad_value_proj,
        grad_state_proj,
        grad_step_proj,
        sums[:4, :128],
        sums[4, :128],
        state_sums[:4],
        state_sums[4],
        head_rows[0, :, 0],
        head_rows[1, :, 0],
        jnp.sum(head_rows[2], axis=1),
        sums[5, :128],
        grad_out_proj,
    )


def solution(mesh):
    in_specs = (
        P("seq", None), P(), P(None, "head"), P(None, "head"), P(), P(None, "head"),
        P(None, "head"), P("head"), P(), P(), P("head"), P("head"), P("head"), P("head"),
        P("head", None), P("seq", None),
    )
    out_specs = (
        P("seq", "head"), P("seq", "head"), P("head"), P(None, "head"), P(None, "head"),
        P("head", None), P(None, "head"), P(None, "head"), P("head"), P(), P(), P("head"),
        P("head"), P("head"), P("head"), P("head", None),
    )
    return jax.shard_map(block, mesh=mesh, in_specs=in_specs, out_specs=out_specs, check_vma=False)
```
